512 devices in a mesh: tm: 64 (over y, x, z_lo), run: 8 (over z_hi, core).
Axes of the slice: x: 4, y: 8, z: 8 (z_hi: 4, z_lo: 2; z = z_hi * 2 + z_lo), core: 2. Of those that a mesh axis runs over, the one named last changes fastest.
Arguments:
- signal: bfloat16 [8, 65536, 256], P('run', 'tm'), may hold values from -6 to 6
- conv_weight: bfloat16 [768, 512], replicated, may hold values from -0.21875 to 0.21875
- conv_bias: float32 [512], replicated, may hold values from -3 to 3
- out_weight: bfloat16 [256, 256], replicated, may hold values from -0.375 to 0.375
- out_bias: float32 [256], replicated, may hold values from -3 to 3
- cotangent: bfloat16 [8, 65536, 256], P('run', 'tm'), may hold values from -8 to 8
Outputs:
- output: bfloat16 [8, 65536, 256], P('run', 'tm')
- grad_signal: bfloat16 [8, 65536, 256], P('run', 'tm')
- grad_conv_weight: float32 [768, 512], replicated
- grad_conv_bias: float32 [512], replicated
- grad_out_weight: float32 [256, 256], replicated
- grad_out_bias: float32 [256], replicated
The draws below stay inside these ranges and needn't reach their ends.
All inputs are finite; a program needn't handle non-finite values.
Results may differ from the reference program's by a relative error of at most 0.0034.
Values may be sent and summed in bfloat16 or wider, within the bound.
A program may use at most 64 MiB of HBM per device.

```python
import jax
import jax.numpy as jnp
from jax import lax

C = 256
DILATION_STEPS = 256
KERNEL_TAPS = 3
STEPS = 65536
RUNS = 8


def draw_cotangent(key, part):
    key_base = jax.random.fold_in(key, 0)
    position = jnp.arange(STEPS, dtype=jnp.float32) / max(STEPS - 1, 1)
    ramp = jnp.exp(jnp.log(3.0) * (position - 0.5))[None, :, None]
    values = jax.random.normal(key_base, (RUNS, STEPS, C), jnp.float32) * ramp
    return jnp.clip(values, -8.0, 8.0).astype(jnp.bfloat16)


def level_of(own_key, shape, shards, low, high):
    loudness, own = 1.0, jax.random.fold_in(own_key, 6)
    for dim, parts in shards:
        heights = jnp.exp(jax.random.uniform(jax.random.fold_in(own, dim), (parts,), jnp.float32, low / len(shards), high / len(shards)))
        loudness = loudness * jnp.repeat(heights, shape[dim] // parts).reshape([-1 if axis == dim else 1 for axis in range(len(shape))])
    return loudness


def normal_values(key, dims, width, reach, cuts=(), kind=jnp.bfloat16):
    level = level_of(key, dims, cuts, -0.22, 0.18) if cuts else 1.0
    values = jax.random.normal(key, dims, jnp.float32) * width * level
    return jnp.minimum(jnp.maximum(values, -reach), reach).astype(kind)


def setup_inputs(seed: int = 0) -> dict:
    arg_keys = jax.random.split(jax.random.key(seed), 7)
    return {
        "signal": normal_values(arg_keys[0], (RUNS, STEPS, C), 1.0, 6.0, ((0, 8), (1, 64))),
        "conv_weight": normal_values(arg_keys[1], (KERNEL_TAPS * C, 2 * C), (KERNEL_TAPS * C) ** -0.5, 0.21875),
        "conv_bias": normal_values(arg_keys[2], (2 * C,), 0.5, 3.0, (), jnp.float32),
        "out_weight": normal_values(arg_keys[3], (C, C), C ** -0.5, 0.375),
        "out_bias": normal_values(arg_keys[4], (C,), 0.5, 3.0, (), jnp.float32),
        "cotangent": draw_cotangent(jax.random.fold_in(arg_keys[6], 71), 0),
    }


def reference(signal, conv_weight, conv_bias, out_weight, out_bias, cotangent):
    receptive_span = (KERNEL_TAPS - 1) * DILATION_STEPS

    def one_run(pair):
        signal_run, cot_run = pair
        total_steps = signal_run.shape[0]
        padded_input = jnp.concatenate([jnp.zeros((receptive_span, C), signal_run.dtype), signal_run], 0)
        tap_stack = jnp.concatenate([padded_input[receptive_span - kernel_tap_index * DILATION_STEPS: receptive_span - kernel_tap_index * DILATION_STEPS + total_steps] for kernel_tap_index in range(KERNEL_TAPS)], 1)
        preact = jnp.dot(tap_stack, conv_weight, preferred_element_type=jnp.float32) + conv_bias
        filtered = jnp.tanh(preact[:, :C])
        gated = jax.nn.sigmoid(preact[:, C:])
        mixed = (filtered * gated).astype(jnp.bfloat16)
        hidden = jnp.dot(mixed, out_weight, preferred_element_type=jnp.float32) + out_bias
        output = (signal_run.astype(jnp.float32) + hidden).astype(jnp.bfloat16)
        dmixed = jnp.dot(cot_run, out_weight.T, preferred_element_type=jnp.float32)
        dpre = jnp.concatenate([dmixed * gated * (1.0 - filtered * filtered), dmixed * filtered * gated * (1.0 - gated)], 1).astype(jnp.bfloat16)
        dstacked = jnp.dot(dpre, conv_weight.T, preferred_element_type=jnp.float32)
        padded_input_gradient = jnp.zeros((receptive_span + total_steps, C), jnp.float32)
        for kernel_tap_index in range(KERNEL_TAPS):
            shifted_slice = dstacked[:, kernel_tap_index * C:(kernel_tap_index + 1) * C]
            padded_input_gradient = padded_input_gradient + jnp.pad(shifted_slice, ((receptive_span - kernel_tap_index * DILATION_STEPS, kernel_tap_index * DILATION_STEPS), (0, 0)))
        grad_run = (cot_run.astype(jnp.float32) + padded_input_gradient[receptive_span:]).astype(jnp.bfloat16)
        grads = (jnp.dot(tap_stack.T, dpre, preferred_element_type=jnp.float32),
                 jnp.sum(dpre.astype(jnp.float32), 0),
                 jnp.dot(mixed.T, cot_run, preferred_element_type=jnp.float32),
                 jnp.sum(cot_run.astype(jnp.float32), 0))
        return output, grad_run, grads

    outputs, grad_signal, grads = lax.map(one_run, (signal, cotangent))
    scale = float(RUNS * STEPS) ** -0.5
    return (outputs, grad_signal, jnp.sum(grads[0], 0) * scale, jnp.sum(grads[1], 0) * scale,
            jnp.sum(grads[2], 0) * scale, jnp.sum(grads[3], 0) * scale)
```

```python
import jax
import jax.numpy as jnp
from jax import lax
from jax.experimental import pallas as pl
from jax.experimental.pallas import tpu as pltpu
from jax.sharding import PartitionSpec as P

MESH = pl.DeviceIdType.MESH
BF = jnp.bfloat16
F32 = jnp.float32
NY, NX, NZ = 8, 4, 8
TM = 64
B = 256
CH = 4
PARTNERS = 32
HI, LO = 128, 136


def nt(a, b):
    return lax.dot_general(a, b, (((1,), (1,)), ((), ())), preferred_element_type=F32)


def tn(a, b):
    return lax.dot_general(a, b, (((0,), (0,)), ((), ())), preferred_element_type=F32)


def nn(a, b):
    return jnp.dot(a, b, preferred_element_type=F32)


def place(y, x, z, c):
    return {"tm": (y * NX + x) * 2 + z % 2, "run": (z // 2) * 2 + c}


def main_kernel(
    scale,
    sig, cw, cb, ow, ob, cot,
    out_ref, gs_ref, res_ref,
    sx, cv, wv, owv, cbv, obv, mixed, dp, grad, gpart, bsend, binc,
    sbuf, cbuf, acc, rbuf, part, agb, agc,
    in_sem, halo_s, halo_r, back_s, back_r,
    cs, cr, rs, rr, ps, pr, gsem, gr, s2, r2,
):
    tm, run = lax.axis_index("tm"), lax.axis_index("run")
    y, x, z, c = tm // 8, (tm // 2) % 4, (run // 2) * 2 + tm % 2, run % 2
    after = {"tm": (tm + 1) % TM, "run": run}
    before = {"tm": (tm + TM - 1) % TM, "run": run}
    sibling = place(y, x, z, 1 - c)

    def member(colour, o):
        if colour == 0:
            zz, xx = (z + o // 4) % NZ, (x + o) % NX
            return place(y, xx, zz, c), zz * 4 + xx
        yy, xx = (y + o // 4) % NY, (x + o) % NX
        return place(yy, xx, z, c), yy * 4 + xx

    def along(colour, o):
        return place((y + o) % NY, x, z, c) if colour == 0 else place(y, x, (z + o) % NZ, c)

    mine = (z * 4 + x, y * 4 + x)
    line = (y, z)

    def remote(src, dst, send, recv, device):
        return pltpu.make_async_remote_copy(
            src_ref=src, dst_ref=dst, send_sem=send, recv_sem=recv, device_id=device, device_id_type=MESH
        )

    def wait_bytes(ref, sem):
        pltpu.make_async_copy(ref, ref, sem).wait()

    loads = [
        pltpu.make_async_copy(sig.at[0], sx.at[pl.ds(2 * B, 4 * B)], in_sem.at[0]),
        pltpu.make_async_copy(cw, wv, in_sem.at[1]),
        pltpu.make_async_copy(cb, cbv, in_sem.at[2]),
        pltpu.make_async_copy(cot.at[0], cv, in_sem.at[3]),
        pltpu.make_async_copy(ow, owv, in_sem.at[4]),
        pltpu.make_async_copy(ob, obv, in_sem.at[5]),
    ]
    for load in loads:
        load.start()

    barrier = pltpu.get_barrier_semaphore()

    def announce(o, carry):
        for colour in range(2):
            pl.semaphore_signal(barrier, inc=1, device_id=member(colour, o)[0], device_id_type=MESH)
        return carry

    lax.fori_loop(1, PARTNERS, announce, 0)
    for device in (after, before, sibling):
        pl.semaphore_signal(barrier, inc=1, device_id=device, device_id_type=MESH)
    for load in loads:
        load.wait()

    def rows(b):
        return pl.ds(b * B, B)

    def activate(b):
        pre = (
            nn(sx[(b + 2) * B : (b + 3) * B], wv[0:B])
            + nn(sx[(b + 1) * B : (b + 2) * B], wv[B : 2 * B])
            + nn(sx[b * B : (b + 1) * B], wv[2 * B : 3 * B])
            + cbv[...]
        )
        f = jnp.tanh(pre[:, :B])
        g = 0.5 * jnp.tanh(0.5 * pre[:, B:]) + 0.5
        mixed[rows(b), :] = (f * g).astype(BF)
        dm = nt(cv[rows(b), :], owv[...])
        dmg = dm * g
        dp[rows(b), 0:B] = (dmg * (1.0 - f * f)).astype(BF)
        dp[rows(b), B : 2 * B] = (dmg * f * (1.0 - g)).astype(BF)

    def tap_term(k, b, n):
        return tn(sx[(b + 2 - k) * B : (b + 2 - k + n) * B], dp[b * B : (b + n) * B])

    def out_term(b, n):
        return tn(mixed[b * B : (b + n) * B], cv[b * B : (b + n) * B])

    def bias_terms(b, n):
        d = jnp.sum(dp[b * B : (b + n) * B].astype(F32), 0, keepdims=True)
        o = jnp.sum(cv[b * B : (b + n) * B].astype(F32), 0, keepdims=True)
        return d, o

    def back(b, k):
        return nt(dp[rows(b), :], wv[k * B : (k + 1) * B])

    def emit_output(b):
        h = nn(mixed[rows(b), :], owv[...]) + obv[...]
        out_ref[rows(b), :] = (sx[(b + 2) * B : (b + 3) * B].astype(F32) + h).astype(BF)

    activate(2)
    pl.semaphore_wait(barrier, 2 * (PARTNERS - 1) + 3)
    halos = []
    for i in (1, 0):
        copy = remote(sx.at[pl.ds((4 + i) * B, B)], sx.at[pl.ds(i * B, B)], halo_s.at[i], halo_r.at[i], after)
        copy.start()
        halos.append(copy)

    activate(3)
    grad[:, 3, HI:B, :] = jnp.zeros((2, B - HI, B), F32)
    for k in range(3):
        t = tap_term(k, 2, 2)
        grad[0, k] = t[:, :B]
        grad[1, k] = t[:, B:]
    t = out_term(2, 2)
    grad[0, 3, 0:HI, :] = t[:HI]
    grad[1, 3, 0:HI, :] = t[HI:]
    d23, o23 = bias_terms(2, 2)
    gpart[0:B, :] = cv[rows(2), :].astype(F32) + back(2, 0) + back(3, 1)
    gpart[B : 2 * B, :] = cv[rows(3), :].astype(F32) + back(3, 0)
    emit_output(2)
    emit_output(3)

    first = tm == 0

    halos[0].wait_recv()

    @pl.when(first)
    def _():
        sx[B : 2 * B, :] = jnp.zeros((B, B), BF)

    activate(1)
    for k in range(3):
        t = tap_term(k, 1, 1)
        grad[0, k] += t[:, :B]
        grad[1, k] += t[:, B:]
    t = out_term(1, 1)
    grad[0, 3, 0:HI, :] += t[:HI]
    grad[1, 3, 0:HI, :] += t[HI:]

    halos[1].wait_recv()

    @pl.when(first)
    def _():
        sx[0:B, :] = jnp.zeros((B, B), BF)

    activate(0)
    pair = []

    def send_half(k):
        copy = remote(sbuf.at[k], cbuf.at[k], cs.at[k], cr.at[k], sibling)
        copy.start()
        pair.append(copy)

    for k in range(3):
        t = tap_term(k, 0, 1)
        grad[0, k] += t[:, :B]
        grad[1, k] += t[:, B:]
        sbuf[k] = grad[1 - c, k].astype(BF)
        send_half(k)
    t = out_term(0, 1)
    grad[0, 3, 0:HI, :] += t[:HI]
    grad[1, 3, 0:HI, :] += t[HI:]
    d01, o01 = bias_terms(0, 2)
    d, o = d23 + d01, o23 + o01
    for h in range(2):
        grad[h, 3, HI : HI + 1, :] = d[:, h * B : (h + 1) * B]
        grad[h, 3, HI + 1 : HI + 2, :] = o
    sbuf[3] = grad[1 - c, 3].astype(BF)
    bias = grad[1 - c, 3, HI:LO, :]
    low = bias - bias.astype(BF).astype(F32)
    sbuf[3, LO : LO + 8, :] = low.astype(BF)
    send_half(3)

    for k in range(CH):
        pair[k].wait_recv()
        s = grad[c, k] + cbuf[k].astype(F32)
        r = s.astype(BF)
        acc[k, 0] = s[:, :128].reshape(PARTNERS, 8, 128).astype(BF)
        acc[k, 1] = s[:, 128:].reshape(PARTNERS, 8, 128).astype(BF)
        if k == 3:
            t = s[HI:LO] + s[LO : LO + 8]
            high = t.astype(BF)
            low = (t - high.astype(F32)).astype(BF)
            for colour in range(2):
                acc[k, colour, HI // 8] = high[:, colour * 128 : (colour + 1) * 128]
                acc[k, colour, LO // 8] = low[:, colour * 128 : (colour + 1) * 128]

        def scatter(o, carry):
            for colour in range(2):
                device, p = member(colour, o)
                remote(acc.at[k, colour, p], rbuf.at[k, colour, o], rs.at[k], rr.at[k, colour], device).start()
            return carry

        lax.fori_loop(1, PARTNERS, scatter, 0)

    bsend[0:B, :] = back(0, 2).astype(BF)
    bsend[B : 2 * B, :] = (back(0, 1) + back(1, 2)).astype(BF)
    backward = remote(bsend, binc, back_s, back_r, before)
    backward.start()
    gs_ref[rows(0), :] = (cv[rows(0), :].astype(F32) + back(0, 0) + back(1, 1) + back(2, 2)).astype(BF)
    gs_ref[rows(1), :] = (cv[rows(1), :].astype(F32) + back(1, 0) + back(2, 1) + back(3, 2)).astype(BF)
    emit_output(0)
    emit_output(1)

    for k in range(CH):
        for colour in range(2):
            wait_bytes(rbuf.at[k, colour, pl.ds(1, PARTNERS - 1)], rr.at[k, colour])
            s = acc[k, colour, mine[colour]].astype(F32)
            s = s + jnp.sum(rbuf[k, colour, 1:PARTNERS].astype(F32), 0)
            part[k, colour, line[colour]] = s

            def spread(o, carry):
                ref = part.at[k, colour, line[colour]]
                remote(ref, ref, ps.at[k], pr.at[k, colour], along(colour, o)).start()
                return carry

            lax.fori_loop(1, 8, spread, 0)

    for k in range(CH):
        for colour in range(2):
            wait_bytes(part.at[k, colour, pl.ds(1, 7)], pr.at[k, colour])
            t = part[k, colour, 0]
            for i in range(1, 8):
                t = t + part[k, colour, i]
            agb[k, colour, mine[colour]] = t.astype(BF)

            def gather(o, carry):
                ref = agb.at[k, colour, mine[colour]]
                remote(ref, ref, gsem.at[k], gr.at[k, colour], member(colour, o)[0]).start()
                return carry

            lax.fori_loop(1, PARTNERS, gather, 0)

    backward.wait_recv()
    last = tm == TM - 1

    @pl.when(last)
    def _():
        binc[...] = jnp.zeros((2 * B, B), BF)

    for i in range(2):
        gs_ref[rows(2 + i), :] = (gpart[rows(i), :] + binc[rows(i), :].astype(F32)).astype(BF)

    swap = []
    for k in range(CH):
        for colour in range(2):
            wait_bytes(agb.at[k, colour, pl.ds(1, PARTNERS - 1)], gr.at[k, colour])
        copy = remote(agb.at[k], agc.at[k], s2.at[k], r2.at[k], sibling)
        copy.start()
        swap.append(copy)
        for colour in range(2):
            v = agb[k, colour].astype(F32).reshape(B, 128) * scale
            res_ref[c, pl.ds(k * B, B), colour * 128 : (colour + 1) * 128] = v
    for k in range(CH):
        swap[k].wait_recv()
        for colour in range(2):
            v = agc[k, colour].astype(F32).reshape(B, 128) * scale
            res_ref[1 - c, pl.ds(k * B, B), colour * 128 : (colour + 1) * 128] = v

    for copy in (*halos, *pair, backward, *swap):
        copy.wait_send()
    for k in range(CH):
        wait_bytes(rbuf.at[k, :, pl.ds(1, PARTNERS - 1)], rs.at[k])
        wait_bytes(part.at[k, :, pl.ds(1, 7)], ps.at[k])
        wait_bytes(agb.at[k, :, pl.ds(1, PARTNERS - 1)], gsem.at[k])


def write_kernel(out, gs, res, out_ref, gs_ref, gcw_ref, gcb_ref, gow_ref, gob_ref, sem):
    copies = [
        pltpu.make_async_copy(out, out_ref.at[0], sem.at[0]),
        pltpu.make_async_copy(gs, gs_ref.at[0], sem.at[1]),
        pltpu.make_async_copy(res.at[0, pl.ds(0, 768)], gcw_ref.at[:, pl.ds(0, B)], sem.at[2]),
        pltpu.make_async_copy(res.at[1, pl.ds(0, 768)], gcw_ref.at[:, pl.ds(B, B)], sem.at[3]),
        pltpu.make_async_copy(res.at[0, pl.ds(768, 128)], gow_ref.at[pl.ds(0, 128)], sem.at[4]),
        pltpu.make_async_copy(res.at[1, pl.ds(768, 128)], gow_ref.at[pl.ds(128, 128)], sem.at[5]),
    ]
    for copy in copies:
        copy.start()
    hi, lo = 768 + HI, 768 + LO
    for h in range(2):
        gcb_ref[0:1, h * B : (h + 1) * B] = res[h, hi : hi + 1, :] + res[h, lo : lo + 1, :]
    gob_ref[...] = res[0, hi + 1 : hi + 2, :] + res[0, lo + 1 : lo + 2, :]
    for copy in copies:
        copy.wait()


def local(signal, conv_weight, conv_bias, out_weight, out_bias, cotangent):
    any_space = pl.BlockSpec(memory_space=pl.ANY)
    vmem = pl.BlockSpec(memory_space=pltpu.VMEM)
    dma = pltpu.SemaphoreType.DMA
    scale = float(8 * 65536) ** -0.5

    def kernel(*refs):
        main_kernel(scale, *refs)

    out, gs, res = pl.pallas_call(
        kernel,
        out_shape=(pltpu.VMEM((4 * B, B), BF), pltpu.VMEM((4 * B, B), BF), pltpu.VMEM((2, CH * B, B), F32)),
        in_specs=[any_space] * 6,
        out_specs=[vmem] * 3,
        scratch_shapes=[
            pltpu.VMEM((6 * B, B), BF),
            pltpu.VMEM((4 * B, B), BF),
            pltpu.VMEM((3 * B, 2 * B), BF),
            pltpu.VMEM((B, B), BF),
            pltpu.VMEM((1, 2 * B), F32),
            pltpu.VMEM((1, B), F32),
            pltpu.VMEM((4 * B, B), BF),
            pltpu.VMEM((4 * B, 2 * B), BF),
            pltpu.VMEM((2, CH, B, B), F32),
            pltpu.VMEM((2 * B, B), F32),
            pltpu.VMEM((2 * B, B), BF),
            pltpu.VMEM((2 * B, B), BF),
            pltpu.VMEM((CH, B, B), BF),
            pltpu.VMEM((CH, B, B), BF),
            pltpu.VMEM((CH, 2, PARTNERS, 8, 128), BF),
            pltpu.VMEM((CH, 2, PARTNERS, 8, 128), BF),
            pltpu.VMEM((CH, 2, 8, 8, 128), F32),
            pltpu.VMEM((CH, 2, PARTNERS, 8, 128), BF),
            pltpu.VMEM((CH, 2, PARTNERS, 8, 128), BF),
            dma((6,)),
            dma((2,)),
            dma((2,)),
            dma,
            dma,
            dma((CH,)),
            dma((CH,)),
            dma((CH,)),
            dma((CH, 2)),
            dma((CH,)),
            dma((CH, 2)),
            dma((CH,)),
            dma((CH, 2)),
            dma((CH,)),
            dma((CH,)),
        ],
        compiler_params=pltpu.CompilerParams(
            collective_id=0, has_side_effects=True, vmem_limit_bytes=40 * 1024 * 1024
        ),
        name="block",
    )(signal, conv_weight, conv_bias.reshape(1, -1), out_weight, out_bias.reshape(1, -1), cotangent)
    output, grad_signal, gcw, gcb, gow, gob = pl.pallas_call(
        write_kernel,
        out_shape=(
            jax.ShapeDtypeStruct((1, 4 * B, B), BF),
            jax.ShapeDtypeStruct((1, 4 * B, B), BF),
            jax.ShapeDtypeStruct((3 * B, 2 * B), F32),
            jax.ShapeDtypeStruct((1, 2 * B), F32),
            jax.ShapeDtypeStruct((B, B), F32),
            jax.ShapeDtypeStruct((1, B), F32),
        ),
        in_specs=[vmem] * 3,
        out_specs=[any_space, any_space, any_space, vmem, any_space, vmem],
        scratch_shapes=[dma((6,))],
        name="write",
    )(out, gs, res)
    return output, grad_signal, gcw, gcb.reshape(-1), gow, gob.reshape(-1)


def solution(mesh):
    placed = (P("run", "tm", None), P(), P(), P(), P(), P("run", "tm", None))
    return jax.shard_map(
        local,
        mesh=mesh,
        in_specs=placed,
        out_specs=(P("run", "tm", None), P("run", "tm", None), P(), P(), P(), P()),
        check_vma=False,
    )
```

```python
import jax
import jax.numpy as jnp
from jax import lax
from jax.experimental import pallas as pl
from jax.experimental.pallas import tpu as pltpu
from jax.sharding import PartitionSpec as P

MESH = pl.DeviceIdType.MESH
BF = jnp.bfloat16
F32 = jnp.float32
NY, NX, NZ = 8, 4, 8
TM = 64
B = 256
CH = 4
PARTNERS = 32
HI, LO = 128, 136


def nt(a, b):
    return lax.dot_general(a, b, (((1,), (1,)), ((), ())), preferred_element_type=F32)


def tn(a, b):
    return lax.dot_general(a, b, (((0,), (0,)), ((), ())), preferred_element_type=F32)


def nn(a, b):
    return jnp.dot(a, b, preferred_element_type=F32)


def rem(a, n):
    return lax.rem(a, jnp.int32(n))


def div(a, n):
    return lax.div(a, jnp.int32(n))


def place(y, x, z, c):
    low = rem(z, 2)
    return {"tm": (y * NX + x) * 2 + low, "run": z - low + c}


def main_kernel(
    scale,
    sig, cw, cb, ow, ob, cot,
    out_ref, gs_ref, res_ref,
    sx, cv, wv, owv, cbv, obv, mixed, dp, grad, gpart, bsend, binc,
    sbuf, cbuf, acc, rbuf, part, agb, agc,
    in_sem, halo_s, halo_r, back_s, back_r,
    cs, cr, rs, rr, ps, pr, gsem, gr, s2, r2,
):
    tm, run = lax.axis_index("tm"), lax.axis_index("run")
    c = rem(run, 2)
    y, x, z = div(tm, 8), rem(div(tm, 2), NX), div(run, 2) * 2 + rem(tm, 2)
    after = {"tm": rem(tm + 1, TM), "run": run}
    before = {"tm": rem(tm + TM - 1, TM), "run": run}
    sibling = place(y, x, z, 1 - c)

    columns = tuple(rem(x + i, NX) for i in range(NX))

    def along(colour, o):
        return place(rem(y + o, NY), x, z, c) if colour == 0 else place(y, x, rem(z + o, NZ), c)

    def plane(visit):
        def line_of(i, first):
            zz, yy = rem(z + i, NZ), rem(y + i, NY)
            for j in range(first, NX):
                xx = columns[j]
                visit(0, i * NX + j, place(y, xx, zz, c), zz * NX + xx)
                visit(1, i * NX + j, place(yy, xx, z, c), yy * NX + xx)

        def step(i, carry):
            line_of(i, 0)
            return carry

        lax.fori_loop(1, 8, step, 0)
        line_of(0, 1)

    mine = (z * 4 + x, y * 4 + x)
    line = (y, z)

    def remote(src, dst, send, recv, device):
        return pltpu.make_async_remote_copy(
            src_ref=src, dst_ref=dst, send_sem=send, recv_sem=recv, device_id=device, device_id_type=MESH
        )

    def wait_bytes(ref, sem):
        pltpu.make_async_copy(ref, ref, sem).wait()

    loads = [
        pltpu.make_async_copy(sig.at[0], sx.at[pl.ds(2 * B, 4 * B)], in_sem.at[0]),
        pltpu.make_async_copy(cw, wv, in_sem.at[1]),
        pltpu.make_async_copy(cb, cbv, in_sem.at[2]),
        pltpu.make_async_copy(cot.at[0], cv, in_sem.at[3]),
        pltpu.make_async_copy(ow, owv, in_sem.at[4]),
        pltpu.make_async_copy(ob, obv, in_sem.at[5]),
    ]
    for load in loads:
        load.start()

    barrier = pltpu.get_barrier_semaphore()

    for device in (after, before, sibling):
        pl.semaphore_signal(barrier, inc=1, device_id=device, device_id_type=MESH)
    plane(lambda colour, slot, device, p: pl.semaphore_signal(barrier, inc=1, device_id=device, device_id_type=MESH))
    pl.semaphore_wait(barrier, 2 * (PARTNERS - 1) + 3)
    halos = []
    for i in (1, 0):
        src = sig.at[0, pl.ds((2 + i) * B, B)]
        copy = remote(src, sx.at[pl.ds(i * B, B)], halo_s.at[i], halo_r.at[i], after)
        copy.start()
        halos.append(copy)
    for load in loads:
        load.wait()

    def rows(b):
        return pl.ds(b * B, B)

    def activate(b):
        pre = (
            nn(sx[(b + 2) * B : (b + 3) * B], wv[0:B])
            + nn(sx[(b + 1) * B : (b + 2) * B], wv[B : 2 * B])
            + nn(sx[b * B : (b + 1) * B], wv[2 * B : 3 * B])
            + cbv[...]
        )
        f = jnp.tanh(pre[:, :B])
        g = 0.5 * jnp.tanh(0.5 * pre[:, B:]) + 0.5
        mixed[rows(b), :] = (f * g).astype(BF)
        dm = nt(cv[rows(b), :], owv[...])
        dmg = dm * g
        dp[rows(b), 0:B] = (dmg * (1.0 - f * f)).astype(BF)
        dp[rows(b), B : 2 * B] = (dmg * f * (1.0 - g)).astype(BF)

    def tap_term(k, b, n):
        return tn(sx[(b + 2 - k) * B : (b + 2 - k + n) * B], dp[b * B : (b + n) * B])

    def out_term(b, n):
        return tn(mixed[b * B : (b + n) * B], cv[b * B : (b + n) * B])

    def bias_terms(b, n):
        d = jnp.sum(dp[b * B : (b + n) * B].astype(F32), 0, keepdims=True)
        o = jnp.sum(cv[b * B : (b + n) * B].astype(F32), 0, keepdims=True)
        return d, o

    def back(b, k):
        return nt(dp[rows(b), :], wv[k * B : (k + 1) * B])

    def emit_output(b):
        h = nn(mixed[rows(b), :], owv[...]) + obv[...]
        out_ref[rows(b), :] = (sx[(b + 2) * B : (b + 3) * B].astype(F32) + h).astype(BF)

    activate(2)
    activate(3)
    grad[:, 3, HI:B, :] = jnp.zeros((2, B - HI, B), F32)
    for k in range(3):
        t = tap_term(k, 2, 2)
        grad[0, k] = t[:, :B]
        grad[1, k] = t[:, B:]
    t = out_term(2, 2)
    grad[0, 3, 0:HI, :] = t[:HI]
    grad[1, 3, 0:HI, :] = t[HI:]
    d23, o23 = bias_terms(2, 2)
    gpart[0:B, :] = cv[rows(2), :].astype(F32) + back(2, 0) + back(3, 1)
    gpart[B : 2 * B, :] = cv[rows(3), :].astype(F32) + back(3, 0)
    emit_output(2)
    emit_output(3)

    first = tm == 0

    halos[0].wait_recv()

    @pl.when(first)
    def _():
        sx[B : 2 * B, :] = jnp.zeros((B, B), BF)

    activate(1)
    for k in range(3):
        t = tap_term(k, 1, 1)
        grad[0, k] += t[:, :B]
        grad[1, k] += t[:, B:]
    t = out_term(1, 1)
    grad[0, 3, 0:HI, :] += t[:HI]
    grad[1, 3, 0:HI, :] += t[HI:]

    halos[1].wait_recv()

    @pl.when(first)
    def _():
        sx[0:B, :] = jnp.zeros((B, B), BF)

    activate(0)
    pair = []

    def send_half(k):
        copy = remote(sbuf.at[k], cbuf.at[k], cs.at[k], cr.at[k], sibling)
        copy.start()
        pair.append(copy)

    for k in range(3):
        t = tap_term(k, 0, 1)
        grad[0, k] += t[:, :B]
        grad[1, k] += t[:, B:]
        sbuf[k] = grad[1 - c, k].astype(BF)
        send_half(k)
    t = out_term(0, 1)
    grad[0, 3, 0:HI, :] += t[:HI]
    grad[1, 3, 0:HI, :] += t[HI:]
    d01, o01 = bias_terms(0, 2)
    d, o = d23 + d01, o23 + o01
    for h in range(2):
        grad[h, 3, HI : HI + 1, :] = d[:, h * B : (h + 1) * B]
        grad[h, 3, HI + 1 : HI + 2, :] = o
    sbuf[3] = grad[1 - c, 3].astype(BF)
    bias = grad[1 - c, 3, HI:LO, :]
    low = bias - bias.astype(BF).astype(F32)
    sbuf[3, LO : LO + 8, :] = low.astype(BF)
    send_half(3)

    for k in range(CH):
        pair[k].wait_recv()
        s = grad[c, k] + cbuf[k].astype(F32)
        acc[k, 0] = s[:, :128].reshape(PARTNERS, 8, 128).astype(BF)
        acc[k, 1] = s[:, 128:].reshape(PARTNERS, 8, 128).astype(BF)
        if k == 3:
            t = s[HI:LO] + s[LO : LO + 8]
            high = t.astype(BF)
            low = (t - high.astype(F32)).astype(BF)
            for colour in range(2):
                acc[k, colour, HI // 8] = high[:, colour * 128 : (colour + 1) * 128]
                acc[k, colour, LO // 8] = low[:, colour * 128 : (colour + 1) * 128]

        plane(
            lambda colour, slot, device, p: remote(
                acc.at[k, colour, p], rbuf.at[k, colour, slot], rs.at[k], rr.at[k, colour], device
            ).start()
        )

    bsend[0:B, :] = back(0, 2).astype(BF)
    bsend[B : 2 * B, :] = (back(0, 1) + back(1, 2)).astype(BF)
    backward = [
        remote(bsend.at[pl.ds(i * 128, 128)], binc.at[pl.ds(i * 128, 128)], back_s.at[i], back_r.at[i], before)
        for i in range(CH)
    ]
    gs_ref[rows(0), :] = (cv[rows(0), :].astype(F32) + back(0, 0) + back(1, 1) + back(2, 2)).astype(BF)
    gs_ref[rows(1), :] = (cv[rows(1), :].astype(F32) + back(1, 0) + back(2, 1) + back(3, 2)).astype(BF)
    emit_output(0)
    emit_output(1)

    for k in range(CH):
        for colour in range(2):
            wait_bytes(rbuf.at[k, colour, pl.ds(1, PARTNERS - 1)], rr.at[k, colour])
            s = acc[k, colour, mine[colour]].astype(F32)
            s = s + jnp.sum(rbuf[k, colour, 1:PARTNERS].astype(F32), 0)
            part[k, colour, line[colour]] = s

            def spread(o, carry):
                ref = part.at[k, colour, line[colour]]
                remote(ref, ref, ps.at[k], pr.at[k, colour], along(colour, o)).start()
                return carry

            lax.fori_loop(1, 8, spread, 0)
        backward[k].start()

    for k in range(CH):
        for colour in range(2):
            wait_bytes(part.at[k, colour, pl.ds(1, 7)], pr.at[k, colour])
            t = part[k, colour, 0]
            for i in range(1, 8):
                t = t + part[k, colour, i]
            agb[k, colour, mine[colour]] = t.astype(BF)

        def gather(colour, slot, device, p):
            ref = agb.at[k, colour, mine[colour]]
            remote(ref, ref, gsem.at[k], gr.at[k, colour], device).start()

        plane(gather)

    def keep(h, k, colour, ref):
        v = ref[k, colour].astype(F32).reshape(B, 128) * scale
        res_ref[h, pl.ds(k * B, B), colour * 128 : (colour + 1) * 128] = v

    swap = []
    for k in range(CH):
        for colour in range(2):
            wait_bytes(agb.at[k, colour, pl.ds(1, PARTNERS - 1)], gr.at[k, colour])
            copy = remote(agb.at[k, colour], agc.at[k, colour], s2.at[k, colour], r2.at[k, colour], sibling)
            copy.start()
            swap.append(copy)
        for colour in range(2):
            keep(c, k, colour, agb)

    for copy in backward:
        copy.wait_recv()

    @pl.when(tm == TM - 1)
    def _():
        binc[...] = jnp.zeros((2 * B, B), BF)

    for i in range(2):
        gs_ref[rows(2 + i), :] = (gpart[rows(i), :] + binc[rows(i), :].astype(F32)).astype(BF)
    for k in range(CH):
        for colour in range(2):
            swap[2 * k + colour].wait_recv()
            keep(1 - c, k, colour, agc)

    for copy in (*halos, *pair, *backward, *swap):
        copy.wait_send()
    for k in range(CH):
        wait_bytes(rbuf.at[k, :, pl.ds(1, PARTNERS - 1)], rs.at[k])
        wait_bytes(part.at[k, :, pl.ds(1, 7)], ps.at[k])
        wait_bytes(agb.at[k, :, pl.ds(1, PARTNERS - 1)], gsem.at[k])


def write_kernel(out, gs, res, out_ref, gs_ref, gcw_ref, gcb_ref, gow_ref, gob_ref, sem):
    copies = [
        pltpu.make_async_copy(out, out_ref.at[0], sem.at[0]),
        pltpu.make_async_copy(gs, gs_ref.at[0], sem.at[1]),
        pltpu.make_async_copy(res.at[0, pl.ds(0, 768)], gcw_ref.at[:, pl.ds(0, B)], sem.at[2]),
        pltpu.make_async_copy(res.at[1, pl.ds(0, 768)], gcw_ref.at[:, pl.ds(B, B)], sem.at[3]),
        pltpu.make_async_copy(res.at[0, pl.ds(768, 128)], gow_ref.at[pl.ds(0, 128)], sem.at[4]),
        pltpu.make_async_copy(res.at[1, pl.ds(768, 128)], gow_ref.at[pl.ds(128, 128)], sem.at[5]),
    ]
    for copy in copies:
        copy.start()
    hi, lo = 768 + HI, 768 + LO
    for h in range(2):
        gcb_ref[0:1, h * B : (h + 1) * B] = res[h, hi : hi + 1, :] + res[h, lo : lo + 1, :]
    gob_ref[...] = res[0, hi + 1 : hi + 2, :] + res[0, lo + 1 : lo + 2, :]
    for copy in copies:
        copy.wait()


def local(signal, conv_weight, conv_bias, out_weight, out_bias, cotangent):
    any_space = pl.BlockSpec(memory_space=pl.ANY)
    vmem = pl.BlockSpec(memory_space=pltpu.VMEM)
    dma = pltpu.SemaphoreType.DMA
    scale = float(8 * 65536) ** -0.5

    def kernel(*refs):
        main_kernel(scale, *refs)

    given = (signal, conv_weight, conv_bias.reshape(1, -1), out_weight, out_bias.reshape(1, -1), cotangent)
    made = pl.pallas_call(
        kernel,
        out_shape=(pltpu.VMEM((4 * B, B), BF), pltpu.VMEM((4 * B, B), BF), pltpu.VMEM((2, CH * B, B), F32)),
        in_specs=[any_space] * 6,
        out_specs=[vmem] * 3,
        scratch_shapes=[
            pltpu.VMEM((6 * B, B), BF),
            pltpu.VMEM((4 * B, B), BF),
            pltpu.VMEM((3 * B, 2 * B), BF),
            pltpu.VMEM((B, B), BF),
            pltpu.VMEM((1, 2 * B), F32),
            pltpu.VMEM((1, B), F32),
            pltpu.VMEM((4 * B, B), BF),
            pltpu.VMEM((4 * B, 2 * B), BF),
            pltpu.VMEM((2, CH, B, B), F32),
            pltpu.VMEM((2 * B, B), F32),
            pltpu.VMEM((2 * B, B), BF),
            pltpu.VMEM((2 * B, B), BF),
            pltpu.VMEM((CH, B, B), BF),
            pltpu.VMEM((CH, B, B), BF),
            pltpu.VMEM((CH, 2, PARTNERS, 8, 128), BF),
            pltpu.VMEM((CH, 2, PARTNERS, 8, 128), BF),
            pltpu.VMEM((CH, 2, 8, 8, 128), F32),
            pltpu.VMEM((CH, 2, PARTNERS, 8, 128), BF),
            pltpu.VMEM((CH, 2, PARTNERS, 8, 128), BF),
            dma((6,)),
            dma((2,)),
            dma((2,)),
            dma((CH,)),
            dma((CH,)),
            dma((CH,)),
            dma((CH,)),
            dma((CH,)),
            dma((CH, 2)),
            dma((CH,)),
            dma((CH, 2)),
            dma((CH,)),
            dma((CH, 2)),
            dma((CH, 2)),
            dma((CH, 2)),
        ],
        compiler_params=pltpu.CompilerParams(
            collective_id=0, has_side_effects=True, vmem_limit_bytes=40 * 1024 * 1024
        ),
        name="block",
    )(*(pltpu.with_memory_space_constraint(v, pltpu.HBM) for v in given))
    output, grad_signal, gcw, gcb, gow, gob = pl.pallas_call(
        write_kernel,
        out_shape=(
            jax.ShapeDtypeStruct((1, 4 * B, B), BF),
            jax.ShapeDtypeStruct((1, 4 * B, B), BF),
            jax.ShapeDtypeStruct((3 * B, 2 * B), F32),
            jax.ShapeDtypeStruct((1, 2 * B), F32),
            jax.ShapeDtypeStruct((B, B), F32),
            jax.ShapeDtypeStruct((1, B), F32),
        ),
        in_specs=[vmem] * 3,
        out_specs=[any_space, any_space, any_space, vmem, any_space, vmem],
        scratch_shapes=[dma((6,))],
        name="write",
    )(*(pltpu.with_memory_space_constraint(v, pltpu.VMEM) for v in made))
    return output, grad_signal, gcw, gcb.reshape(-1), gow, gob.reshape(-1)


def solution(mesh):
    placed = (P("run", "tm", None), P(), P(), P(), P(), P("run", "tm", None))
    return jax.shard_map(
        local,
        mesh=mesh,
        in_specs=placed,
        out_specs=(P("run", "tm", None), P("run", "tm", None), P(), P(), P(), P()),
        check_vma=False,
    )
```

```python
import jax
import jax.numpy as jnp
from jax import lax
from jax.experimental import pallas as pl
from jax.experimental.pallas import tpu as pltpu
from jax.sharding import PartitionSpec as P

MESH = pl.DeviceIdType.MESH
BF = jnp.bfloat16
F32 = jnp.float32
NY, NX, NZ = 8, 4, 8
TM = 64
B = 256
CH = 4
PARTNERS = 32
HI, LO = 128, 136
USED = (32, 32, 32, 18)


def nt(a, b):
    return lax.dot_general(a, b, (((1,), (1,)), ((), ())), preferred_element_type=F32)


def tn(a, b):
    return lax.dot_general(a, b, (((0,), (0,)), ((), ())), preferred_element_type=F32)


def nn(a, b):
    return jnp.dot(a, b, preferred_element_type=F32)


def rem(a, n):
    return lax.rem(a, jnp.int32(n))


def div(a, n):
    return lax.div(a, jnp.int32(n))


def place(y, x, z, c):
    low = rem(z, 2)
    return {"tm": (y * NX + x) * 2 + low, "run": z - low + c}


def main_kernel(
    scale,
    sig, cw, cb, ow, ob, cot,
    out_ref, gs_ref, res_ref,
    sx, cv, wv, owv, cbv, obv, pre0, pre1, dmix, mixed, dp, grad, gpart, bsend, binc,
    sbuf, cbuf, acc, rbuf, part, agb, agc,
    in_sem, known, halo_s, halo_r, back_s, back_r,
    cs, cr, rs, rr, ps, pr, gsem, gr, s2, r2,
):
    tm, run = lax.axis_index("tm"), lax.axis_index("run")
    c = rem(run, 2)
    y, x, z = div(tm, 8), rem(div(tm, 2), NX), div(run, 2) * 2 + rem(tm, 2)
    after = {"tm": rem(tm + 1, TM), "run": run}
    before = {"tm": rem(tm + TM - 1, TM), "run": run}
    sibling = place(y, x, z, 1 - c)

    columns = tuple(rem(x + i, NX) for i in range(NX))

    def along(colour, o):
        return place(rem(y + o, NY), x, z, c) if colour == 0 else place(y, x, rem(z + o, NZ), c)

    def plane(visit):
        def line_of(i, first):
            zz, yy = rem(z + i, NZ), rem(y + i, NY)
            for j in range(first, NX):
                xx = columns[j]
                visit(0, i * NX + j, place(y, xx, zz, c), xx * 8 + zz)
                visit(1, i * NX + j, place(yy, xx, z, c), xx * 8 + yy)

        def step(i, carry):
            line_of(i, 0)
            return carry

        lax.fori_loop(1, 8, step, 0)
        line_of(0, 1)

    mine = (x * 8 + z, x * 8 + y)
    line = (y, z)

    def remote(src, dst, send, recv, device):
        return pltpu.make_async_remote_copy(
            src_ref=src, dst_ref=dst, send_sem=send, recv_sem=recv, device_id=device, device_id_type=MESH
        )

    def wait_bytes(ref, sem):
        pltpu.make_async_copy(ref, ref, sem).wait()

    loads = [
        pltpu.make_async_copy(sig.at[0], sx.at[pl.ds(2 * B, 4 * B)], in_sem.at[0]),
        pltpu.make_async_copy(cw, wv, in_sem.at[1]),
        pltpu.make_async_copy(cb, cbv, in_sem.at[2]),
        pltpu.make_async_copy(cot.at[0], cv, in_sem.at[3]),
        pltpu.make_async_copy(ow, owv, in_sem.at[4]),
        pltpu.make_async_copy(ob, obv, in_sem.at[5]),
    ]
    for load in loads:
        load.start()

    barrier = pltpu.get_barrier_semaphore()

    row = [place(y, columns[j], z, c) for j in range(1, NX)]
    near = [along(colour, i) for i in (2, 6, 1, 7) for colour in range(2)] + row

    def tell(semaphore, devices):
        for device in devices:
            pl.semaphore_signal(semaphore, inc=1, device_id=device, device_id_type=MESH)

    tell(barrier, [after, before, *near, sibling])
    pl.semaphore_wait(barrier, len(near) + 3)
    halos = []
    for i in (1, 0):
        src = sig.at[0, pl.ds((2 + i) * B, B)]
        copy = remote(src, sx.at[pl.ds(i * B, B)], halo_s.at[i], halo_r.at[i], after)
        copy.start()
        halos.append(copy)
    tell(known.at[0], near)
    for load in loads:
        load.wait()

    def rows(b):
        return pl.ds(b * B, B)

    def pre_term(b, k):
        return nn(sx[(b + 2 - k) * B : (b + 3 - k) * B], wv[k * B : (k + 1) * B])

    def activate(b, pre, dm):
        f = jnp.tanh(pre[:, :B])
        g = 0.5 * jnp.tanh(0.5 * pre[:, B:]) + 0.5
        mixed[rows(b), :] = (f * g).astype(BF)
        dmg = dm * g
        dp[rows(b), 0:B] = (dmg * (1.0 - f * f)).astype(BF)
        dp[rows(b), B : 2 * B] = (dmg * f * (1.0 - g)).astype(BF)

    def mixed_back(b):
        return nt(cv[rows(b), :], owv[...])

    def tap_term(k, b, n):
        return tn(sx[(b + 2 - k) * B : (b + 2 - k + n) * B], dp[b * B : (b + n) * B])

    def out_term(b, n):
        return tn(mixed[b * B : (b + n) * B], cv[b * B : (b + n) * B])

    def bias_terms(b, n):
        d = jnp.sum(dp[b * B : (b + n) * B].astype(F32), 0, keepdims=True)
        o = jnp.sum(cv[b * B : (b + n) * B].astype(F32), 0, keepdims=True)
        return d, o

    def back(b, k):
        return nt(dp[rows(b), :], wv[k * B : (k + 1) * B])

    def emit_output(b):
        h = nn(mixed[rows(b), :], owv[...]) + obv[...]
        out_ref[rows(b), :] = (sx[(b + 2) * B : (b + 3) * B].astype(F32) + h).astype(BF)

    for b in (2, 3):
        activate(b, pre_term(b, 0) + pre_term(b, 1) + pre_term(b, 2) + cbv[...], mixed_back(b))
    pl.semaphore_wait(known.at[0], len(near))
    tell(known.at[1], row)
    grad[:, 3, HI:B, :] = jnp.zeros((2, B - HI, B), F32)
    for k in range(3):
        t = tap_term(k, 2, 2)
        grad[0, k] = t[:, :B]
        grad[1, k] = t[:, B:]
    t = out_term(2, 2)
    grad[0, 3, 0:HI, :] = t[:HI]
    grad[1, 3, 0:HI, :] = t[HI:]
    d23, o23 = bias_terms(2, 2)
    gpart[0:B, :] = cv[rows(2), :].astype(F32) + back(2, 0) + back(3, 1)
    gpart[B : 2 * B, :] = cv[rows(3), :].astype(F32) + back(3, 0)
    emit_output(2)
    emit_output(3)
    pre1[...] = pre_term(1, 0) + pre_term(1, 1) + cbv[...]
    pre0[...] = pre_term(0, 0) + cbv[...]
    dmix[...] = mixed_back(0)

    first = tm == 0

    halos[0].wait_recv()

    @pl.when(first)
    def _():
        sx[B : 2 * B, :] = jnp.zeros((B, B), BF)

    activate(1, pre1[...] + pre_term(1, 2), mixed_back(1))
    pre0[...] += pre_term(0, 1)
    for k in range(3):
        t = tap_term(k, 1, 1)
        grad[0, k] += t[:, :B]
        grad[1, k] += t[:, B:]
    t = out_term(1, 1)
    grad[0, 3, 0:HI, :] += t[:HI]
    grad[1, 3, 0:HI, :] += t[HI:]

    halos[1].wait_recv()

    @pl.when(first)
    def _():
        sx[0:B, :] = jnp.zeros((B, B), BF)

    activate(0, pre0[...] + pre_term(0, 2), dmix[...])
    pair = []

    def send_half(k):
        copy = remote(sbuf.at[k], cbuf.at[k], cs.at[k], cr.at[k], sibling)
        copy.start()
        pair.append(copy)

    for k in range(3):
        t = tap_term(k, 0, 1)
        grad[0, k] += t[:, :B]
        grad[1, k] += t[:, B:]
        sbuf[k] = grad[1 - c, k].astype(BF)
        send_half(k)
    t = out_term(0, 1)
    grad[0, 3, 0:HI, :] += t[:HI]
    grad[1, 3, 0:HI, :] += t[HI:]
    d01, o01 = bias_terms(0, 2)
    d, o = d23 + d01, o23 + o01
    for h in range(2):
        grad[h, 3, HI : HI + 1, :] = d[:, h * B : (h + 1) * B]
        grad[h, 3, HI + 1 : HI + 2, :] = o
    sbuf[3] = grad[1 - c, 3].astype(BF)
    bias = grad[1 - c, 3, HI:LO, :]
    low = bias - bias.astype(BF).astype(F32)
    sbuf[3, LO : LO + 8, :] = low.astype(BF)
    send_half(3)

    for k in range(CH):
        pair[k].wait_recv()
        s = grad[c, k] + cbuf[k].astype(F32)
        acc[k, 0] = s[:, :128].reshape(PARTNERS, 8, 128).astype(BF)
        acc[k, 1] = s[:, 128:].reshape(PARTNERS, 8, 128).astype(BF)
        if k == 3:
            t = s[HI:LO] + s[LO : LO + 8]
            high = t.astype(BF)
            low = (t - high.astype(F32)).astype(BF)
            for colour in range(2):
                acc[k, colour, HI // 8] = high[:, colour * 128 : (colour + 1) * 128]
                acc[k, colour, LO // 8] = low[:, colour * 128 : (colour + 1) * 128]

        def scatter(colour, slot, device, p):
            copy = remote(
                acc.at[k, colour, p], rbuf.at[k, colour, slot], rs.at[k, colour], rr.at[k, colour], device
            )
            if USED[k] == PARTNERS:
                copy.start()
            else:
                pl.when(p < USED[k])(copy.start)

        if k == 0:
            pl.semaphore_wait(known.at[1], NX - 1)
        plane(scatter)

    bsend[0:B, :] = back(0, 2).astype(BF)
    bsend[B : 2 * B, :] = (back(0, 1) + back(1, 2)).astype(BF)
    backward = [
        remote(bsend.at[pl.ds(i * 128, 128)], binc.at[pl.ds(i * 128, 128)], back_s.at[i], back_r.at[i], before)
        for i in range(CH)
    ]
    gs_ref[rows(0), :] = (cv[rows(0), :].astype(F32) + back(0, 0) + back(1, 1) + back(2, 2)).astype(BF)
    gs_ref[rows(1), :] = (cv[rows(1), :].astype(F32) + back(1, 0) + back(2, 1) + back(3, 2)).astype(BF)
    emit_output(0)
    emit_output(1)

    def if_mine(k, colour, work):
        if USED[k] == PARTNERS:
            work()
        else:
            pl.when(mine[colour] < USED[k])(work)

    def wait_others(k, colour, ref, sem):
        n = USED[k]
        if n == PARTNERS:
            wait_bytes(ref.at[pl.ds(0, n - 1)], sem)
        else:
            pl.when(mine[colour] < n)(lambda: wait_bytes(ref.at[pl.ds(0, n - 1)], sem))
            pl.when(mine[colour] >= n)(lambda: wait_bytes(ref.at[pl.ds(0, n)], sem))

    for k in range(CH):
        for colour in range(2):

            def reduce_plane():
                wait_bytes(rbuf.at[k, colour, pl.ds(1, PARTNERS - 1)], rr.at[k, colour])
                s = acc[k, colour, mine[colour]].astype(F32)
                s = s + jnp.sum(rbuf[k, colour, 1:PARTNERS].astype(F32), 0)
                part[k, colour, line[colour]] = s

                def spread(o, carry):
                    ref = part.at[k, colour, line[colour]]
                    remote(ref, ref, ps.at[k, colour], pr.at[k, colour], along(colour, o)).start()
                    return carry

                lax.fori_loop(1, 8, spread, 0)

            if_mine(k, colour, reduce_plane)
        backward[k].start()

    for k in range(CH):
        for colour in range(2):

            def finish():
                wait_bytes(part.at[k, colour, pl.ds(1, 7)], pr.at[k, colour])
                t = part[k, colour, 0]
                for i in range(1, 8):
                    t = t + part[k, colour, i]
                agb[k, colour, mine[colour]] = t.astype(BF)

            if_mine(k, colour, finish)

        def gather(colour, slot, device, p):
            ref = agb.at[k, colour, mine[colour]]
            copy = remote(ref, ref, gsem.at[k, colour], gr.at[k, colour], device)
            if_mine(k, colour, copy.start)

        plane(gather)

    def keep(h, k, colour, ref):
        n = USED[k]
        v = ref[k, colour, 0:n].astype(F32).reshape(n * 8, 128) * scale
        res_ref[h, pl.ds(k * B, n * 8), colour * 128 : (colour + 1) * 128] = v

    swap = []
    for k in range(CH):
        used = pl.ds(0, USED[k])
        for colour in range(2):
            wait_others(k, colour, agb.at[k, colour], gr.at[k, colour])
            copy = remote(
                agb.at[k, colour, used], agc.at[k, colour, used], s2.at[k, colour], r2.at[k, colour], sibling
            )
            copy.start()
            swap.append(copy)
        for colour in range(2):
            keep(c, k, colour, agb)

    for copy in backward:
        copy.wait_recv()

    @pl.when(tm == TM - 1)
    def _():
        binc[...] = jnp.zeros((2 * B, B), BF)

    for i in range(2):
        gs_ref[rows(2 + i), :] = (gpart[rows(i), :] + binc[rows(i), :].astype(F32)).astype(BF)
    for k in range(CH):
        for colour in range(2):
            swap[2 * k + colour].wait_recv()
            keep(1 - c, k, colour, agc)

    for copy in (*halos, *pair, *backward, *swap):
        copy.wait_send()
    for k in range(CH):
        for colour in range(2):
            wait_others(k, colour, rbuf.at[k, colour], rs.at[k, colour])

            def sent():
                wait_bytes(part.at[k, colour, pl.ds(1, 7)], ps.at[k, colour])
                wait_bytes(agb.at[k, colour, pl.ds(1, PARTNERS - 1)], gsem.at[k, colour])

            if_mine(k, colour, sent)


def write_kernel(out, gs, res, out_ref, gs_ref, gcw_ref, gcb_ref, gow_ref, gob_ref, sem):
    copies = [
        pltpu.make_async_copy(out, out_ref.at[0], sem.at[0]),
        pltpu.make_async_copy(gs, gs_ref.at[0], sem.at[1]),
        pltpu.make_async_copy(res.at[0, pl.ds(0, 768)], gcw_ref.at[:, pl.ds(0, B)], sem.at[2]),
        pltpu.make_async_copy(res.at[1, pl.ds(0, 768)], gcw_ref.at[:, pl.ds(B, B)], sem.at[3]),
        pltpu.make_async_copy(res.at[0, pl.ds(768, 128)], gow_ref.at[pl.ds(0, 128)], sem.at[4]),
        pltpu.make_async_copy(res.at[1, pl.ds(768, 128)], gow_ref.at[pl.ds(128, 128)], sem.at[5]),
    ]
    for copy in copies:
        copy.start()
    hi, lo = 768 + HI, 768 + LO
    for h in range(2):
        gcb_ref[0:1, h * B : (h + 1) * B] = res[h, hi : hi + 1, :] + res[h, lo : lo + 1, :]
    gob_ref[...] = res[0, hi + 1 : hi + 2, :] + res[0, lo + 1 : lo + 2, :]
    for copy in copies:
        copy.wait()


def local(signal, conv_weight, conv_bias, out_weight, out_bias, cotangent):
    any_space = pl.BlockSpec(memory_space=pl.ANY)
    vmem = pl.BlockSpec(memory_space=pltpu.VMEM)
    dma = pltpu.SemaphoreType.DMA
    scale = float(8 * 65536) ** -0.5

    def kernel(*refs):
        main_kernel(scale, *refs)

    given = (signal, conv_weight, conv_bias.reshape(1, -1), out_weight, out_bias.reshape(1, -1), cotangent)
    made = pl.pallas_call(
        kernel,
        out_shape=(pltpu.VMEM((4 * B, B), BF), pltpu.VMEM((4 * B, B), BF), pltpu.VMEM((2, CH * B, B), F32)),
        in_specs=[any_space] * 6,
        out_specs=[vmem] * 3,
        scratch_shapes=[
            pltpu.VMEM((6 * B, B), BF),
            pltpu.VMEM((4 * B, B), BF),
            pltpu.VMEM((3 * B, 2 * B), BF),
            pltpu.VMEM((B, B), BF),
            pltpu.VMEM((1, 2 * B), F32),
            pltpu.VMEM((1, B), F32),
            pltpu.VMEM((B, 2 * B), F32),
            pltpu.VMEM((B, 2 * B), F32),
            pltpu.VMEM((B, B), F32),
            pltpu.VMEM((4 * B, B), BF),
            pltpu.VMEM((4 * B, 2 * B), BF),
            pltpu.VMEM((2, CH, B, B), F32),
            pltpu.VMEM((2 * B, B), F32),
            pltpu.VMEM((2 * B, B), BF),
            pltpu.VMEM((2 * B, B), BF),
            pltpu.VMEM((CH, B, B), BF),
            pltpu.VMEM((CH, B, B), BF),
            pltpu.VMEM((CH, 2, PARTNERS, 8, 128), BF),
            pltpu.VMEM((CH, 2, PARTNERS, 8, 128), BF),
            pltpu.VMEM((CH, 2, 8, 8, 128), F32),
            pltpu.VMEM((CH, 2, PARTNERS, 8, 128), BF),
            pltpu.VMEM((CH, 2, PARTNERS, 8, 128), BF),
            dma((6,)),
            pltpu.SemaphoreType.REGULAR((2,)),
            dma((2,)),
            dma((2,)),
            dma((CH,)),
            dma((CH,)),
            dma((CH,)),
            dma((CH,)),
            dma((CH, 2)),
            dma((CH, 2)),
            dma((CH, 2)),
            dma((CH, 2)),
            dma((CH, 2)),
            dma((CH, 2)),
            dma((CH, 2)),
            dma((CH, 2)),
        ],
        compiler_params=pltpu.CompilerParams(
            collective_id=0, has_side_effects=True, vmem_limit_bytes=40 * 1024 * 1024
        ),
        name="block",
    )(*(pltpu.with_memory_space_constraint(v, pltpu.HBM) for v in given))
    output, grad_signal, gcw, gcb, gow, gob = pl.pallas_call(
        write_kernel,
        out_shape=(
            jax.ShapeDtypeStruct((1, 4 * B, B), BF),
            jax.ShapeDtypeStruct((1, 4 * B, B), BF),
            jax.ShapeDtypeStruct((3 * B, 2 * B), F32),
            jax.ShapeDtypeStruct((1, 2 * B), F32),
            jax.ShapeDtypeStruct((B, B), F32),
            jax.ShapeDtypeStruct((1, B), F32),
        ),
        in_specs=[vmem] * 3,
        out_specs=[any_space, any_space, any_space, vmem, any_space, vmem],
        scratch_shapes=[dma((6,))],
        name="write",
    )(*(pltpu.with_memory_space_constraint(v, pltpu.VMEM) for v in made))
    return output, grad_signal, gcw, gcb.reshape(-1), gow, gob.reshape(-1)


def solution(mesh):
    placed = (P("run", "tm", None), P(), P(), P(), P(), P("run", "tm", None))
    return jax.shard_map(
        local,
        mesh=mesh,
        in_specs=placed,
        out_specs=(P("run", "tm", None), P("run", "tm", None), P(), P(), P(), P()),
        check_vma=False,
    )
```

```python
import jax
import jax.numpy as jnp
from jax import lax
from jax.experimental import pallas as pl
from jax.experimental.pallas import tpu as pltpu
from jax.sharding import PartitionSpec as P

MESH = pl.DeviceIdType.MESH
BF = jnp.bfloat16
F32 = jnp.float32
NY, NX, NZ = 8, 4, 8
TM = 64
B = 256
CH = 4
PARTNERS = 32
HI, LO = 128, 136
USED = (32, 32, 32, 18)


def nt(a, b):
    return lax.dot_general(a, b, (((1,), (1,)), ((), ())), preferred_element_type=F32)


def tn(a, b):
    return lax.dot_general(a, b, (((0,), (0,)), ((), ())), preferred_element_type=F32)


def nn(a, b):
    return jnp.dot(a, b, preferred_element_type=F32)


def rem(a, n):
    return lax.rem(a, jnp.int32(n))


def div(a, n):
    return lax.div(a, jnp.int32(n))


def place(y, x, z, c):
    low = rem(z, 2)
    return {"tm": (y * NX + x) * 2 + low, "run": z - low + c}


def main_kernel(
    scale,
    sig, cw, cb, ow, ob, cot,
    out_ref, gs_ref, res_ref,
    sx, cv, wv, owv, cbv, obv, pre0, pre1, dmix, mixed, dp, grad, gpart, bsend, binc,
    sbuf, cbuf, acc, rbuf, part, agb, agc,
    in_sem, known, halo_s, halo_r, back_s, back_r,
    cs, cr, rs, rr, ps, pr, gsem, gr, s2, r2,
):
    tm, run = lax.axis_index("tm"), lax.axis_index("run")
    c = rem(run, 2)
    y, x, z = div(tm, 8), rem(div(tm, 2), NX), div(run, 2) * 2 + rem(tm, 2)
    after = {"tm": rem(tm + 1, TM), "run": run}
    before = {"tm": rem(tm + TM - 1, TM), "run": run}
    sibling = place(y, x, z, 1 - c)

    columns = tuple(rem(x + i, NX) for i in range(NX))

    def along(colour, o):
        return place(rem(y + o, NY), x, z, c) if colour == 0 else place(y, x, rem(z + o, NZ), c)

    def plane(visit):
        def line_of(i, first):
            zz, yy = rem(z + i, NZ), rem(y + i, NY)
            for j in (2, 1, 3, 0)[: NX - first]:
                xx = columns[j]
                visit(0, i * NX + j, place(y, xx, zz, c), xx * 8 + zz)
                visit(1, i * NX + j, place(yy, xx, z, c), xx * 8 + yy)

        def step(t, carry):
            line_of(4 + (2 * rem(t, 2) - 1) * div(t + 1, 2), 0)
            return carry

        lax.fori_loop(0, 7, step, 0)
        line_of(0, 1)

    mine = (x * 8 + z, x * 8 + y)
    line = (y, z)

    def remote(src, dst, send, recv, device):
        return pltpu.make_async_remote_copy(
            src_ref=src, dst_ref=dst, send_sem=send, recv_sem=recv, device_id=device, device_id_type=MESH
        )

    def wait_bytes(ref, sem):
        pltpu.make_async_copy(ref, ref, sem).wait()

    loads = [
        pltpu.make_async_copy(sig.at[0], sx.at[pl.ds(2 * B, 4 * B)], in_sem.at[0]),
        pltpu.make_async_copy(cw, wv, in_sem.at[1]),
        pltpu.make_async_copy(cb, cbv, in_sem.at[2]),
        pltpu.make_async_copy(cot.at[0], cv, in_sem.at[3]),
        pltpu.make_async_copy(ow, owv, in_sem.at[4]),
        pltpu.make_async_copy(ob, obv, in_sem.at[5]),
    ]
    for load in loads:
        load.start()

    barrier = pltpu.get_barrier_semaphore()

    row = [place(y, columns[j], z, c) for j in range(1, NX)]
    near = [along(colour, i) for i in (2, 6, 1, 7) for colour in range(2)] + row

    def tell(semaphore, devices):
        for device in devices:
            pl.semaphore_signal(semaphore, inc=1, device_id=device, device_id_type=MESH)

    tell(barrier, [after, before, *near, sibling])
    pl.semaphore_wait(barrier, len(near) + 3)
    halos = []
    for i in (1, 0):
        src = sig.at[0, pl.ds((2 + i) * B, B)]
        copy = remote(src, sx.at[pl.ds(i * B, B)], halo_s.at[i], halo_r.at[i], after)
        copy.start()
        halos.append(copy)
    tell(known.at[0], near)
    for load in loads:
        load.wait()

    def rows(b):
        return pl.ds(b * B, B)

    def pre_term(b, k):
        return nn(sx[(b + 2 - k) * B : (b + 3 - k) * B], wv[k * B : (k + 1) * B])

    def activate(b, pre, dm):
        f = jnp.tanh(pre[:, :B])
        g = 0.5 * jnp.tanh(0.5 * pre[:, B:]) + 0.5
        mixed[rows(b), :] = (f * g).astype(BF)
        dmg = dm * g
        dp[rows(b), 0:B] = (dmg * (1.0 - f * f)).astype(BF)
        dp[rows(b), B : 2 * B] = (dmg * f * (1.0 - g)).astype(BF)

    def mixed_back(b):
        return nt(cv[rows(b), :], owv[...])

    def tap_term(k, b, n):
        return tn(sx[(b + 2 - k) * B : (b + 2 - k + n) * B], dp[b * B : (b + n) * B])

    def out_term(b, n):
        return tn(mixed[b * B : (b + n) * B], cv[b * B : (b + n) * B])

    def bias_terms(b, n):
        d = jnp.sum(dp[b * B : (b + n) * B].astype(F32), 0, keepdims=True)
        o = jnp.sum(cv[b * B : (b + n) * B].astype(F32), 0, keepdims=True)
        return d, o

    def back(b, k):
        return nt(dp[rows(b), :], wv[k * B : (k + 1) * B])

    def emit_output(b):
        h = nn(mixed[rows(b), :], owv[...]) + obv[...]
        out_ref[rows(b), :] = (sx[(b + 2) * B : (b + 3) * B].astype(F32) + h).astype(BF)

    for b in (2, 3):
        activate(b, pre_term(b, 0) + pre_term(b, 1) + pre_term(b, 2) + cbv[...], mixed_back(b))
    pl.semaphore_wait(known.at[0], len(near))
    tell(known.at[1], row)
    grad[:, 3, HI:B, :] = jnp.zeros((2, B - HI, B), F32)
    for k in range(3):
        t = tap_term(k, 2, 2)
        grad[0, k] = t[:, :B]
        grad[1, k] = t[:, B:]
    t = out_term(2, 2)
    grad[0, 3, 0:HI, :] = t[:HI]
    grad[1, 3, 0:HI, :] = t[HI:]
    d23, o23 = bias_terms(2, 2)
    gpart[0:B, :] = cv[rows(2), :].astype(F32) + back(2, 0) + back(3, 1)
    gpart[B : 2 * B, :] = cv[rows(3), :].astype(F32) + back(3, 0)
    emit_output(2)
    emit_output(3)
    pre1[...] = pre_term(1, 0) + pre_term(1, 1) + cbv[...]
    pre0[...] = pre_term(0, 0) + cbv[...]
    dmix[...] = mixed_back(0)

    first = tm == 0

    halos[0].wait_recv()

    @pl.when(first)
    def _():
        sx[B : 2 * B, :] = jnp.zeros((B, B), BF)

    activate(1, pre1[...] + pre_term(1, 2), mixed_back(1))
    pre0[...] += pre_term(0, 1)
    for k in range(3):
        t = tap_term(k, 1, 1)
        grad[0, k] += t[:, :B]
        grad[1, k] += t[:, B:]
    t = out_term(1, 1)
    grad[0, 3, 0:HI, :] += t[:HI]
    grad[1, 3, 0:HI, :] += t[HI:]

    halos[1].wait_recv()

    @pl.when(first)
    def _():
        sx[0:B, :] = jnp.zeros((B, B), BF)

    activate(0, pre0[...] + pre_term(0, 2), dmix[...])
    pair = []

    def send_half(k):
        copy = remote(sbuf.at[k], cbuf.at[k], cs.at[k], cr.at[k], sibling)
        copy.start()
        pair.append(copy)

    for k in range(3):
        t = tap_term(k, 0, 1)
        grad[0, k] += t[:, :B]
        grad[1, k] += t[:, B:]
        sbuf[k] = grad[1 - c, k].astype(BF)
        send_half(k)
    t = out_term(0, 1)
    grad[0, 3, 0:HI, :] += t[:HI]
    grad[1, 3, 0:HI, :] += t[HI:]
    d01, o01 = bias_terms(0, 2)
    d, o = d23 + d01, o23 + o01
    for h in range(2):
        grad[h, 3, HI : HI + 1, :] = d[:, h * B : (h + 1) * B]
        grad[h, 3, HI + 1 : HI + 2, :] = o
    sbuf[3] = grad[1 - c, 3].astype(BF)
    bias = grad[1 - c, 3, HI:LO, :]
    low = bias - bias.astype(BF).astype(F32)
    sbuf[3, LO : LO + 8, :] = low.astype(BF)
    send_half(3)

    for k in range(CH):
        pair[k].wait_recv()
        s = grad[c, k] + cbuf[k].astype(F32)
        acc[k, 0] = s[:, :128].reshape(PARTNERS, 8, 128).astype(BF)
        acc[k, 1] = s[:, 128:].reshape(PARTNERS, 8, 128).astype(BF)
        if k == 3:
            t = s[HI:LO] + s[LO : LO + 8]
            high = t.astype(BF)
            low = (t - high.astype(F32)).astype(BF)
            for colour in range(2):
                acc[k, colour, HI // 8] = high[:, colour * 128 : (colour + 1) * 128]
                acc[k, colour, LO // 8] = low[:, colour * 128 : (colour + 1) * 128]

        def scatter(colour, slot, device, p):
            copy = remote(
                acc.at[k, colour, p], rbuf.at[k, colour, slot], rs.at[k, colour], rr.at[k, colour], device
            )
            if USED[k] == PARTNERS:
                copy.start()
            else:
                pl.when(p < USED[k])(copy.start)

        if k == 0:
            pl.semaphore_wait(known.at[1], NX - 1)
        plane(scatter)

    bsend[0:B, :] = back(0, 2).astype(BF)
    bsend[B : 2 * B, :] = (back(0, 1) + back(1, 2)).astype(BF)
    backward = [
        remote(bsend.at[pl.ds(i * 128, 128)], binc.at[pl.ds(i * 128, 128)], back_s.at[i], back_r.at[i], before)
        for i in range(CH)
    ]
    gs_ref[rows(0), :] = (cv[rows(0), :].astype(F32) + back(0, 0) + back(1, 1) + back(2, 2)).astype(BF)
    gs_ref[rows(1), :] = (cv[rows(1), :].astype(F32) + back(1, 0) + back(2, 1) + back(3, 2)).astype(BF)
    emit_output(0)
    emit_output(1)

    def if_mine(k, colour, work):
        if USED[k] == PARTNERS:
            work()
        else:
            pl.when(mine[colour] < USED[k])(work)

    def wait_others(k, colour, ref, sem):
        n = USED[k]
        if n == PARTNERS:
            wait_bytes(ref.at[pl.ds(0, n - 1)], sem)
        else:
            pl.when(mine[colour] < n)(lambda: wait_bytes(ref.at[pl.ds(0, n - 1)], sem))
            pl.when(mine[colour] >= n)(lambda: wait_bytes(ref.at[pl.ds(0, n)], sem))

    for k in range(CH):
        for colour in range(2):

            def reduce_plane():
                wait_bytes(rbuf.at[k, colour, pl.ds(1, PARTNERS - 1)], rr.at[k, colour])
                s = acc[k, colour, mine[colour]].astype(F32)
                s = s + jnp.sum(rbuf[k, colour, 1:PARTNERS].astype(F32), 0)
                part[k, colour, line[colour]] = s

                def spread(o, carry):
                    ref = part.at[k, colour, line[colour]]
                    remote(ref, ref, ps.at[k, colour], pr.at[k, colour], along(colour, o)).start()
                    return carry

                lax.fori_loop(1, 8, spread, 0)

            if_mine(k, colour, reduce_plane)

    for k in range(CH):
        for colour in range(2):

            def finish():
                wait_bytes(part.at[k, colour, pl.ds(1, 7)], pr.at[k, colour])
                t = part[k, colour, 0]
                for i in range(1, 8):
                    t = t + part[k, colour, i]
                agb[k, colour, mine[colour]] = t.astype(BF)

            if_mine(k, colour, finish)

        def gather(colour, slot, device, p):
            ref = agb.at[k, colour, mine[colour]]
            copy = remote(ref, ref, gsem.at[k, colour], gr.at[k, colour], device)
            if_mine(k, colour, copy.start)

        plane(gather)
    for copy in backward:
        copy.start()

    def keep(h, k, colour, ref):
        n = USED[k]
        v = ref[k, colour, 0:n].astype(F32).reshape(n * 8, 128) * scale
        res_ref[h, pl.ds(k * B, n * 8), colour * 128 : (colour + 1) * 128] = v

    def gathered(k, colour):
        if_mine(k, colour, lambda: wait_bytes(agb.at[k, colour, pl.ds(1, PARTNERS - 1)], gsem.at[k, colour]))

    for copy in (*halos, *pair):
        copy.wait_send()
    for k in range(CH):
        for colour in range(2):
            wait_others(k, colour, rbuf.at[k, colour], rs.at[k, colour])
            if_mine(k, colour, lambda: wait_bytes(part.at[k, colour, pl.ds(1, 7)], ps.at[k, colour]))

    swap = []

    def keep_other(k):
        for colour in range(2):
            swap[2 * k + colour].wait_recv()
            keep(1 - c, k, colour, agc)

    for k in range(CH):
        used = pl.ds(0, USED[k])
        for colour in range(2):
            wait_others(k, colour, agb.at[k, colour], gr.at[k, colour])
            copy = remote(
                agb.at[k, colour, used], agc.at[k, colour, used], s2.at[k, colour], r2.at[k, colour], sibling
            )
            copy.start()
            swap.append(copy)
        for colour in range(2):
            keep(c, k, colour, agb)
            if k < CH - 1:
                gathered(k, colour)
        if k > 0:
            keep_other(k - 1)
    keep_other(CH - 1)

    for copy in backward:
        copy.wait_recv()

    @pl.when(tm == TM - 1)
    def _():
        binc[...] = jnp.zeros((2 * B, B), BF)

    for i in range(2):
        gs_ref[rows(2 + i), :] = (gpart[rows(i), :] + binc[rows(i), :].astype(F32)).astype(BF)
    for copy in (*backward, *swap):
        copy.wait_send()
    for colour in range(2):
        gathered(CH - 1, colour)


def write_kernel(out, gs, res, out_ref, gs_ref, gcw_ref, gcb_ref, gow_ref, gob_ref, cbias, obias, sem):
    copies = [
        pltpu.make_async_copy(res.at[0, pl.ds(0, 768)], gcw_ref.at[:, pl.ds(0, B)], sem.at[2]),
        pltpu.make_async_copy(res.at[1, pl.ds(0, 768)], gcw_ref.at[:, pl.ds(B, B)], sem.at[3]),
        pltpu.make_async_copy(out, out_ref.at[0], sem.at[0]),
        pltpu.make_async_copy(gs, gs_ref.at[0], sem.at[1]),
        pltpu.make_async_copy(res.at[0, pl.ds(768, 128)], gow_ref.at[pl.ds(0, 128)], sem.at[4]),
        pltpu.make_async_copy(res.at[1, pl.ds(768, 128)], gow_ref.at[pl.ds(128, 128)], sem.at[5]),
    ]
    for copy in copies:
        copy.start()
    hi, lo = 768 + HI, 768 + LO
    for h in range(2):
        cbias[0:1, h * B : (h + 1) * B] = res[h, hi : hi + 1, :] + res[h, lo : lo + 1, :]
    obias[...] = res[0, hi + 1 : hi + 2, :] + res[0, lo + 1 : lo + 2, :]
    small = [
        pltpu.make_async_copy(cbias, gcb_ref, sem.at[6]),
        pltpu.make_async_copy(obias, gob_ref, sem.at[7]),
    ]
    for copy in small:
        copy.start()
    for copy in copies + small:
        copy.wait()


def local(signal, conv_weight, conv_bias, out_weight, out_bias, cotangent):
    any_space = pl.BlockSpec(memory_space=pl.ANY)
    vmem = pl.BlockSpec(memory_space=pltpu.VMEM)
    dma = pltpu.SemaphoreType.DMA
    scale = float(8 * 65536) ** -0.5

    def kernel(*refs):
        main_kernel(scale, *refs)

    given = (signal, conv_weight, conv_bias.reshape(1, -1), out_weight, out_bias.reshape(1, -1), cotangent)
    made = pl.pallas_call(
        kernel,
        out_shape=(pltpu.VMEM((4 * B, B), BF), pltpu.VMEM((4 * B, B), BF), pltpu.VMEM((2, CH * B, B), F32)),
        in_specs=[any_space] * 6,
        out_specs=[vmem] * 3,
        scratch_shapes=[
            pltpu.VMEM((6 * B, B), BF),
            pltpu.VMEM((4 * B, B), BF),
            pltpu.VMEM((3 * B, 2 * B), BF),
            pltpu.VMEM((B, B), BF),
            pltpu.VMEM((1, 2 * B), F32),
            pltpu.VMEM((1, B), F32),
            pltpu.VMEM((B, 2 * B), F32),
            pltpu.VMEM((B, 2 * B), F32),
            pltpu.VMEM((B, B), F32),
            pltpu.VMEM((4 * B, B), BF),
            pltpu.VMEM((4 * B, 2 * B), BF),
            pltpu.VMEM((2, CH, B, B), F32),
            pltpu.VMEM((2 * B, B), F32),
            pltpu.VMEM((2 * B, B), BF),
            pltpu.VMEM((2 * B, B), BF),
            pltpu.VMEM((CH, B, B), BF),
            pltpu.VMEM((CH, B, B), BF),
            pltpu.VMEM((CH, 2, PARTNERS, 8, 128), BF),
            pltpu.VMEM((CH, 2, PARTNERS, 8, 128), BF),
            pltpu.VMEM((CH, 2, 8, 8, 128), F32),
            pltpu.VMEM((CH, 2, PARTNERS, 8, 128), BF),
            pltpu.VMEM((CH, 2, PARTNERS, 8, 128), BF),
            dma((6,)),
            pltpu.SemaphoreType.REGULAR((2,)),
            dma((2,)),
            dma((2,)),
            dma((CH,)),
            dma((CH,)),
            dma((CH,)),
            dma((CH,)),
            dma((CH, 2)),
            dma((CH, 2)),
            dma((CH, 2)),
            dma((CH, 2)),
            dma((CH, 2)),
            dma((CH, 2)),
            dma((CH, 2)),
            dma((CH, 2)),
        ],
        compiler_params=pltpu.CompilerParams(
            collective_id=0, has_side_effects=True, vmem_limit_bytes=40 * 1024 * 1024
        ),
        name="block",
    )(*(pltpu.with_memory_space_constraint(v, pltpu.HBM) for v in given))
    output, grad_signal, gcw, gcb, gow, gob = pl.pallas_call(
        write_kernel,
        out_shape=(
            jax.ShapeDtypeStruct((1, 4 * B, B), BF),
            jax.ShapeDtypeStruct((1, 4 * B, B), BF),
            jax.ShapeDtypeStruct((3 * B, 2 * B), F32),
            jax.ShapeDtypeStruct((1, 2 * B), F32),
            jax.ShapeDtypeStruct((B, B), F32),
            jax.ShapeDtypeStruct((1, B), F32),
        ),
        in_specs=[vmem] * 3,
        out_specs=[any_space] * 6,
        scratch_shapes=[pltpu.VMEM((1, 2 * B), F32), pltpu.VMEM((1, B), F32), dma((8,))],
        name="write",
    )(*(pltpu.with_memory_space_constraint(v, pltpu.VMEM) for v in made))
    return output, grad_signal, gcw, gcb.reshape(-1), gow, gob.reshape(-1)


def solution(mesh):
    placed = (P("run", "tm", None), P(), P(), P(), P(), P("run", "tm", None))
    return jax.shard_map(
        local,
        mesh=mesh,
        in_specs=placed,
        out_specs=(P("run", "tm", None), P("run", "tm", None), P(), P(), P(), P()),
        check_vma=False,
    )
```

```python
import jax
import jax.numpy as jnp
from jax import lax
from jax.experimental import pallas as pl
from jax.experimental.pallas import tpu as pltpu
from jax.sharding import PartitionSpec as P

MESH = pl.DeviceIdType.MESH
BF = jnp.bfloat16
F32 = jnp.float32
NY, NX, NZ = 8, 4, 8
TM = 64
B = 256
CH = 4
PARTNERS = 32
HI, LO = 128, 136
USED = (32, 32, 32, 18)


def nt(a, b):
    return lax.dot_general(a, b, (((1,), (1,)), ((), ())), preferred_element_type=F32)


def tn(a, b):
    return lax.dot_general(a, b, (((0,), (0,)), ((), ())), preferred_element_type=F32)


def nn(a, b):
    return jnp.dot(a, b, preferred_element_type=F32)


def rem(a, n):
    return lax.rem(a, jnp.int32(n))


def div(a, n):
    return lax.div(a, jnp.int32(n))


def place(y, x, z, c):
    low = rem(z, 2)
    return {"tm": (y * NX + x) * 2 + low, "run": z - low + c}


def main_kernel(
    scale,
    sig, cw, cb, ow, ob, cot,
    out_ref, gs_ref, res_ref,
    sx, cv, wv, owv, cbv, obv, pre0, pre1, dmix, mixed, dp, grad, gpart, bsend, binc,
    sbuf, cbuf, acc, rbuf, part, agb, agc,
    in_sem, known, halo_s, halo_r, back_s, back_r,
    cs, cr, rs, rr, ps, pr, gsem, gr, s2, r2,
):
    tm, run = lax.axis_index("tm"), lax.axis_index("run")
    c = rem(run, 2)
    y, x, z = div(tm, 8), rem(div(tm, 2), NX), div(run, 2) * 2 + rem(tm, 2)
    after = {"tm": rem(tm + 1, TM), "run": run}
    before = {"tm": rem(tm + TM - 1, TM), "run": run}
    sibling = place(y, x, z, 1 - c)

    columns = tuple(rem(x + i, NX) for i in range(NX))

    def along(colour, o):
        return place(rem(y + o, NY), x, z, c) if colour == 0 else place(y, x, rem(z + o, NZ), c)

    def plane(visit):
        def line_of(i, first):
            zz, yy = rem(z + i, NZ), rem(y + i, NY)
            for j in (2, 1, 3, 0)[: NX - first]:
                xx = columns[j]
                visit(0, i * NX + j, place(y, xx, zz, c), xx * 8 + zz)
                visit(1, i * NX + j, place(yy, xx, z, c), xx * 8 + yy)

        def step(t, carry):
            line_of(4 + (2 * rem(t, 2) - 1) * div(t + 1, 2), 0)
            return carry

        lax.fori_loop(0, 7, step, 0)
        line_of(0, 1)

    mine = (x * 8 + z, x * 8 + y)
    line = (y, z)

    def remote(src, dst, send, recv, device):
        return pltpu.make_async_remote_copy(
            src_ref=src, dst_ref=dst, send_sem=send, recv_sem=recv, device_id=device, device_id_type=MESH
        )

    def wait_bytes(ref, sem):
        pltpu.make_async_copy(ref, ref, sem).wait()

    loads = [
        pltpu.make_async_copy(sig.at[0], sx.at[pl.ds(2 * B, 4 * B)], in_sem.at[0]),
        pltpu.make_async_copy(cw, wv, in_sem.at[1]),
        pltpu.make_async_copy(cb, cbv, in_sem.at[2]),
        pltpu.make_async_copy(cot.at[0], cv, in_sem.at[3]),
        pltpu.make_async_copy(ow, owv, in_sem.at[4]),
        pltpu.make_async_copy(ob, obv, in_sem.at[5]),
    ]
    for load in loads:
        load.start()

    barrier = pltpu.get_barrier_semaphore()

    row = [place(y, columns[j], z, c) for j in range(1, NX)]
    near = [along(colour, i) for i in (2, 6, 1, 7) for colour in range(2)] + row

    def tell(semaphore, devices):
        for device in devices:
            pl.semaphore_signal(semaphore, inc=1, device_id=device, device_id_type=MESH)

    tell(barrier, [after, before, *near, sibling])
    pl.semaphore_wait(barrier, len(near) + 3)
    halos = []
    for i in (1, 0):
        src = sig.at[0, pl.ds((2 + i) * B, B)]
        copy = remote(src, sx.at[pl.ds(i * B, B)], halo_s.at[i], halo_r.at[i], after)
        copy.start()
        halos.append(copy)
    tell(known.at[0], near)
    for load in loads:
        load.wait()

    def rows(b):
        return pl.ds(b * B, B)

    def pre_term(b, k):
        return nn(sx[(b + 2 - k) * B : (b + 3 - k) * B], wv[k * B : (k + 1) * B])

    def activate(b, pre, dm):
        f = jnp.tanh(pre[:, :B])
        g = 0.5 * jnp.tanh(0.5 * pre[:, B:]) + 0.5
        mixed[rows(b), :] = (f * g).astype(BF)
        dmg = dm * g
        dp[rows(b), 0:B] = (dmg * (1.0 - f * f)).astype(BF)
        dp[rows(b), B : 2 * B] = (dmg * f * (1.0 - g)).astype(BF)

    def mixed_back(b):
        return nt(cv[rows(b), :], owv[...])

    def tap_term(k, b, n):
        return tn(sx[(b + 2 - k) * B : (b + 2 - k + n) * B], dp[b * B : (b + n) * B])

    def out_term(b, n):
        return tn(mixed[b * B : (b + n) * B], cv[b * B : (b + n) * B])

    def bias_terms(b, n):
        d = jnp.sum(dp[b * B : (b + n) * B].astype(F32), 0, keepdims=True)
        o = jnp.sum(cv[b * B : (b + n) * B].astype(F32), 0, keepdims=True)
        return d, o

    def back(b, k):
        return nt(dp[rows(b), :], wv[k * B : (k + 1) * B])

    def emit_output(b):
        h = nn(mixed[rows(b), :], owv[...]) + obv[...]
        out_ref[rows(b), :] = (sx[(b + 2) * B : (b + 3) * B].astype(F32) + h).astype(BF)

    for b in (2, 3):
        activate(b, pre_term(b, 0) + pre_term(b, 1) + pre_term(b, 2) + cbv[...], mixed_back(b))
    pl.semaphore_wait(known.at[0], len(near))
    tell(known.at[1], row)
    grad[:, 3, HI:B, :] = jnp.zeros((2, B - HI, B), F32)
    for k in range(3):
        t = tap_term(k, 2, 2)
        grad[0, k] = t[:, :B]
        grad[1, k] = t[:, B:]
    t = out_term(2, 2)
    grad[0, 3, 0:HI, :] = t[:HI]
    grad[1, 3, 0:HI, :] = t[HI:]
    d23, o23 = bias_terms(2, 2)
    pre1[...] = pre_term(1, 0) + pre_term(1, 1) + cbv[...]
    pre0[...] = pre_term(0, 0) + cbv[...]
    dmix[...] = mixed_back(0)

    first = tm == 0

    halos[0].wait_recv()

    @pl.when(first)
    def _():
        sx[B : 2 * B, :] = jnp.zeros((B, B), BF)

    activate(1, pre1[...] + pre_term(1, 2), mixed_back(1))
    pre0[...] += pre_term(0, 1)
    for k in range(3):
        t = tap_term(k, 1, 1)
        grad[0, k] += t[:, :B]
        grad[1, k] += t[:, B:]
    t = out_term(1, 1)
    grad[0, 3, 0:HI, :] += t[:HI]
    grad[1, 3, 0:HI, :] += t[HI:]

    d1, o1 = bias_terms(1, 1)

    halos[1].wait_recv()

    @pl.when(first)
    def _():
        sx[0:B, :] = jnp.zeros((B, B), BF)

    activate(0, pre0[...] + pre_term(0, 2), dmix[...])
    pair = []

    def send_half(k):
        copy = remote(sbuf.at[k], cbuf.at[k], cs.at[k], cr.at[k], sibling)
        copy.start()
        pair.append(copy)

    for k in range(3):
        t = tap_term(k, 0, 1)
        grad[0, k] += t[:, :B]
        grad[1, k] += t[:, B:]
        sbuf[k] = grad[1 - c, k].astype(BF)
        send_half(k)
    t = out_term(0, 1)
    grad[0, 3, 0:HI, :] += t[:HI]
    grad[1, 3, 0:HI, :] += t[HI:]
    d0, o0 = bias_terms(0, 1)
    d, o = d23 + d1 + d0, o23 + o1 + o0
    for h in range(2):
        grad[h, 3, HI : HI + 1, :] = d[:, h * B : (h + 1) * B]
        grad[h, 3, HI + 1 : HI + 2, :] = o
    sbuf[3] = grad[1 - c, 3].astype(BF)
    bias = grad[1 - c, 3, HI:LO, :]
    low = bias - bias.astype(BF).astype(F32)
    sbuf[3, LO : LO + 8, :] = low.astype(BF)
    send_half(3)

    for k in range(CH):
        pair[k].wait_recv()
        s = grad[c, k] + cbuf[k].astype(F32)
        acc[k, 0] = s[:, :128].reshape(PARTNERS, 8, 128).astype(BF)
        acc[k, 1] = s[:, 128:].reshape(PARTNERS, 8, 128).astype(BF)
        if k == 3:
            t = s[HI:LO] + s[LO : LO + 8]
            high = t.astype(BF)
            low = (t - high.astype(F32)).astype(BF)
            for colour in range(2):
                acc[k, colour, HI // 8] = high[:, colour * 128 : (colour + 1) * 128]
                acc[k, colour, LO // 8] = low[:, colour * 128 : (colour + 1) * 128]

        def scatter(colour, slot, device, p):
            copy = remote(
                acc.at[k, colour, p], rbuf.at[k, colour, slot], rs.at[k, colour], rr.at[k, colour], device
            )
            if USED[k] == PARTNERS:
                copy.start()
            else:
                pl.when(p < USED[k])(copy.start)

        if k == 0:
            pl.semaphore_wait(known.at[1], NX - 1)
        plane(scatter)

    bsend[0:B, :] = back(0, 2).astype(BF)
    bsend[B : 2 * B, :] = (back(0, 1) + back(1, 2)).astype(BF)
    backward = [
        remote(bsend.at[pl.ds(i * 128, 128)], binc.at[pl.ds(i * 128, 128)], back_s.at[i], back_r.at[i], before)
        for i in range(CH)
    ]
    gs_ref[rows(0), :] = (cv[rows(0), :].astype(F32) + back(0, 0) + back(1, 1) + back(2, 2)).astype(BF)
    gs_ref[rows(1), :] = (cv[rows(1), :].astype(F32) + back(1, 0) + back(2, 1) + back(3, 2)).astype(BF)
    emit_output(0)
    emit_output(1)
    gpart[0:B, :] = cv[rows(2), :].astype(F32) + back(2, 0) + back(3, 1)
    gpart[B : 2 * B, :] = cv[rows(3), :].astype(F32) + back(3, 0)
    emit_output(2)
    emit_output(3)

    def if_mine(k, colour, work):
        if USED[k] == PARTNERS:
            work()
        else:
            pl.when(mine[colour] < USED[k])(work)

    def wait_others(k, colour, ref, sem):
        n = USED[k]
        if n == PARTNERS:
            wait_bytes(ref.at[pl.ds(0, n - 1)], sem)
        else:
            pl.when(mine[colour] < n)(lambda: wait_bytes(ref.at[pl.ds(0, n - 1)], sem))
            pl.when(mine[colour] >= n)(lambda: wait_bytes(ref.at[pl.ds(0, n)], sem))

    for k in range(CH):
        for colour in range(2):

            def reduce_plane():
                wait_bytes(rbuf.at[k, colour, pl.ds(1, PARTNERS - 1)], rr.at[k, colour])
                s = acc[k, colour, mine[colour]].astype(F32)
                s = s + jnp.sum(rbuf[k, colour, 1:PARTNERS].astype(F32), 0)
                part[k, colour, line[colour]] = s

                def spread(o, carry):
                    ref = part.at[k, colour, line[colour]]
                    remote(ref, ref, ps.at[k, colour], pr.at[k, colour], along(colour, o)).start()
                    return carry

                lax.fori_loop(1, 8, spread, 0)

            if_mine(k, colour, reduce_plane)

    for k in range(CH):
        for colour in range(2):

            def finish():
                wait_bytes(part.at[k, colour, pl.ds(1, 7)], pr.at[k, colour])
                t = part[k, colour, 0]
                for i in range(1, 8):
                    t = t + part[k, colour, i]
                agb[k, colour, mine[colour]] = t.astype(BF)

            if_mine(k, colour, finish)

        def gather(colour, slot, device, p):
            ref = agb.at[k, colour, mine[colour]]
            copy = remote(ref, ref, gsem.at[k, colour], gr.at[k, colour], device)
            if_mine(k, colour, copy.start)

        plane(gather)
    for copy in backward:
        copy.start()

    def keep(h, k, colour, ref):
        n = USED[k]
        v = ref[k, colour, 0:n].astype(F32).reshape(n * 8, 128) * scale
        res_ref[h, pl.ds(k * B, n * 8), colour * 128 : (colour + 1) * 128] = v

    def gathered(k, colour):
        if_mine(k, colour, lambda: wait_bytes(agb.at[k, colour, pl.ds(1, PARTNERS - 1)], gsem.at[k, colour]))

    for copy in (*halos, *pair):
        copy.wait_send()
    for k in range(CH):
        for colour in range(2):
            wait_others(k, colour, rbuf.at[k, colour], rs.at[k, colour])
            if_mine(k, colour, lambda: wait_bytes(part.at[k, colour, pl.ds(1, 7)], ps.at[k, colour]))

    swap = []

    def keep_other(k):
        for colour in range(2):
            swap[2 * k + colour].wait_recv()
            keep(1 - c, k, colour, agc)

    for k in range(CH):
        used = pl.ds(0, USED[k])
        for colour in range(2):
            wait_others(k, colour, agb.at[k, colour], gr.at[k, colour])
            copy = remote(
                agb.at[k, colour, used], agc.at[k, colour, used], s2.at[k, colour], r2.at[k, colour], sibling
            )
            copy.start()
            swap.append(copy)
        for colour in range(2):
            keep(c, k, colour, agb)
            if k < CH - 1:
                gathered(k, colour)
        if k > 0:
            keep_other(k - 1)
    keep_other(CH - 1)

    for copy in backward:
        copy.wait_recv()

    @pl.when(tm == TM - 1)
    def _():
        binc[...] = jnp.zeros((2 * B, B), BF)

    for i in range(2):
        gs_ref[rows(2 + i), :] = (gpart[rows(i), :] + binc[rows(i), :].astype(F32)).astype(BF)
    for copy in (*backward, *swap):
        copy.wait_send()
    for colour in range(2):
        gathered(CH - 1, colour)


def write_kernel(out, gs, res, out_ref, gs_ref, gcw_ref, gcb_ref, gow_ref, gob_ref, cbias, obias, sem):
    copies = [
        pltpu.make_async_copy(res.at[0, pl.ds(0, 768)], gcw_ref.at[:, pl.ds(0, B)], sem.at[2]),
        pltpu.make_async_copy(res.at[1, pl.ds(0, 768)], gcw_ref.at[:, pl.ds(B, B)], sem.at[3]),
        pltpu.make_async_copy(out, out_ref.at[0], sem.at[0]),
        pltpu.make_async_copy(gs, gs_ref.at[0], sem.at[1]),
        pltpu.make_async_copy(res.at[0, pl.ds(768, 128)], gow_ref.at[pl.ds(0, 128)], sem.at[4]),
        pltpu.make_async_copy(res.at[1, pl.ds(768, 128)], gow_ref.at[pl.ds(128, 128)], sem.at[5]),
    ]
    for copy in copies:
        copy.start()
    hi, lo = 768 + HI, 768 + LO
    for h in range(2):
        cbias[0:1, h * B : (h + 1) * B] = res[h, hi : hi + 1, :] + res[h, lo : lo + 1, :]
    obias[...] = res[0, hi + 1 : hi + 2, :] + res[0, lo + 1 : lo + 2, :]
    small = [
        pltpu.make_async_copy(cbias, gcb_ref, sem.at[6]),
        pltpu.make_async_copy(obias, gob_ref, sem.at[7]),
    ]
    for copy in small:
        copy.start()
    for copy in copies + small:
        copy.wait()


def local(signal, conv_weight, conv_bias, out_weight, out_bias, cotangent):
    any_space = pl.BlockSpec(memory_space=pl.ANY)
    vmem = pl.BlockSpec(memory_space=pltpu.VMEM)
    dma = pltpu.SemaphoreType.DMA
    scale = float(8 * 65536) ** -0.5

    def kernel(*refs):
        main_kernel(scale, *refs)

    given = (signal, conv_weight, conv_bias.reshape(1, -1), out_weight, out_bias.reshape(1, -1), cotangent)
    made = pl.pallas_call(
        kernel,
        out_shape=(pltpu.VMEM((4 * B, B), BF), pltpu.VMEM((4 * B, B), BF), pltpu.VMEM((2, CH * B, B), F32)),
        in_specs=[any_space] * 6,
        out_specs=[vmem] * 3,
        scratch_shapes=[
            pltpu.VMEM((6 * B, B), BF),
            pltpu.VMEM((4 * B, B), BF),
            pltpu.VMEM((3 * B, 2 * B), BF),
            pltpu.VMEM((B, B), BF),
            pltpu.VMEM((1, 2 * B), F32),
            pltpu.VMEM((1, B), F32),
            pltpu.VMEM((B, 2 * B), F32),
            pltpu.VMEM((B, 2 * B), F32),
            pltpu.VMEM((B, B), F32),
            pltpu.VMEM((4 * B, B), BF),
            pltpu.VMEM((4 * B, 2 * B), BF),
            pltpu.VMEM((2, CH, B, B), F32),
            pltpu.VMEM((2 * B, B), F32),
            pltpu.VMEM((2 * B, B), BF),
            pltpu.VMEM((2 * B, B), BF),
            pltpu.VMEM((CH, B, B), BF),
            pltpu.VMEM((CH, B, B), BF),
            pltpu.VMEM((CH, 2, PARTNERS, 8, 128), BF),
            pltpu.VMEM((CH, 2, PARTNERS, 8, 128), BF),
            pltpu.VMEM((CH, 2, 8, 8, 128), F32),
            pltpu.VMEM((CH, 2, PARTNERS, 8, 128), BF),
            pltpu.VMEM((CH, 2, PARTNERS, 8, 128), BF),
            dma((6,)),
            pltpu.SemaphoreType.REGULAR((2,)),
            dma((2,)),
            dma((2,)),
            dma((CH,)),
            dma((CH,)),
            dma((CH,)),
            dma((CH,)),
            dma((CH, 2)),
            dma((CH, 2)),
            dma((CH, 2)),
            dma((CH, 2)),
            dma((CH, 2)),
            dma((CH, 2)),
            dma((CH, 2)),
            dma((CH, 2)),
        ],
        compiler_params=pltpu.CompilerParams(
            collective_id=0, has_side_effects=True, vmem_limit_bytes=40 * 1024 * 1024
        ),
        name="block",
    )(*(pltpu.with_memory_space_constraint(v, pltpu.HBM) for v in given))
    output, grad_signal, gcw, gcb, gow, gob = pl.pallas_call(
        write_kernel,
        out_shape=(
            jax.ShapeDtypeStruct((1, 4 * B, B), BF),
            jax.ShapeDtypeStruct((1, 4 * B, B), BF),
            jax.ShapeDtypeStruct((3 * B, 2 * B), F32),
            jax.ShapeDtypeStruct((1, 2 * B), F32),
            jax.ShapeDtypeStruct((B, B), F32),
            jax.ShapeDtypeStruct((1, B), F32),
        ),
        in_specs=[vmem] * 3,
        out_specs=[any_space] * 6,
        scratch_shapes=[pltpu.VMEM((1, 2 * B), F32), pltpu.VMEM((1, B), F32), dma((8,))],
        name="write",
    )(*(pltpu.with_memory_space_constraint(v, pltpu.VMEM) for v in made))
    return output, grad_signal, gcw, gcb.reshape(-1), gow, gob.reshape(-1)


def solution(mesh):
    placed = (P("run", "tm", None), P(), P(), P(), P(), P("run", "tm", None))
    return jax.shard_map(
        local,
        mesh=mesh,
        in_specs=placed,
        out_specs=(P("run", "tm", None), P("run", "tm", None), P(), P(), P(), P()),
        check_vma=False,
    )
```
